32 devices in a mesh: fsdp: 4 (over y, x), seq: 4 (over z), tp: 2 (over core).
Axes of the slice: x: 2, y: 2, z: 4, core: 2. Of those that a mesh axis runs over, the one named last changes fastest.
Arguments:
- tokens: bfloat16 [1024, 8192], P('seq'), may hold values from -6 to 6
- norm_gain: float32 [8192], replicated, may hold values from 0.1 to 1.9
- in_weight: bfloat16 [3, 8192, 8192], P(None, 'seq', ('fsdp', 'tp')), may hold values from -0.0625 to 0.0625
- short_filter: float32 [7, 3, 8192], P(None, None, ('fsdp', 'tp')), may hold values from -2.4 to 2.4
- long_filter: float32 [128, 512], P(None, ('fsdp', 'tp')), may hold values from -0.5 to 0.5
- out_weight: bfloat16 [8192, 8192], P(('fsdp', 'tp'), 'seq'), may hold values from -0.0625 to 0.0625
- segment_ids: int32 [1024], replicated, may hold values from 0 to 7, never falling along the last dimension, each value on 1 to 256 neighbouring positions
Outputs:
- block_out: bfloat16 [1024, 8192], P('seq', ('fsdp', 'tp'))
The draws below stay inside these ranges and needn't reach their ends.
Inputs may be any that keep to these rules, and one draw needn't show every extreme that they name: `segment_ids`: segment numbers never fall along the sequence and each is used; a segment covers at most 256 positions and one covers exactly 256.
All inputs are finite; a program needn't handle non-finite values.
Results may differ from the reference program's by a relative error of at most 0.0087.
Values may be sent and summed in bfloat16 or wider, within the bound.
No kernel may reach another device: no remote copies, remote signals or barrier semaphores. Data moves between devices by JAX's collectives and lax.ppermute only.
A program may use at most 192 MiB of HBM per device.

```python
import math
import jax
import jax.numpy as jnp
import numpy as np
from jax import lax

D = 8192
C = 8192
GROUP = 16
KS = 7
KL = 128
TOK_DEV = 256
LENGTH = 1024
SEGS = 8
NF = 512


def block_scale(rng, extent, split, low, high):
    level = 1.0
    for axis_at, parts in split:
        steps = jax.random.uniform(jax.random.fold_in(jax.random.fold_in(rng, 6), axis_at), (parts,), jnp.float32, low / len(split), high / len(split))
        level = level * jnp.repeat(jnp.exp(steps), extent[axis_at] // parts).reshape((-1,) + (1,) * (len(extent) - 1 - axis_at))
    return level


def length_profile(count, total, reach, skew):
    loads = [(1 << 20) // math.isqrt(rank ** skew) + 1 for rank in range(2, count + 1)]
    spare, holding = total - reach - (count - 1), [1] * (count - 1)
    while spare > 0:
        candidates = [i for i in range(count - 1) if holding[i] < reach]
        mass, remaining = sum([loads[i] for i in candidates]), spare
        for i in candidates:
            extra = min(reach - holding[i], max(1, remaining * loads[i] // mass), spare)
            holding[i] = holding[i] + extra
            spare = spare - extra
    return np.array([reach] + holding)


def ragged(own_key, amount, total, bound, slope):
    if amount == 2:
        one = jax.random.randint(own_key, (), max(1, total - bound), min(bound, total - 1) + 1)
        return jnp.stack([one, total - one])
    sizes = jnp.asarray(length_profile(amount, total, bound, slope), jnp.int32)
    pairs = (amount - 1) // 2
    donor, taker = sizes[1:1 + 2 * pairs:2], sizes[2:2 + 2 * pairs:2]
    margin = jnp.minimum(donor - 1, bound - taker)
    passed = jax.random.randint(jax.random.fold_in(own_key, 1), (pairs,), 0, 1 << 20) % (margin + 1)
    sizes = sizes.at[1:1 + 2 * pairs:2].set(donor - passed).at[2:2 + 2 * pairs:2].set(taker + passed)
    return sizes[jax.random.permutation(jax.random.fold_in(own_key, 2), amount)]


def centred(rng, extent, scale, most, pieces=(), held_as=jnp.bfloat16):
    entries = jax.random.normal(rng, extent, jnp.float32) * scale
    if len(pieces) > 0:
        entries = block_scale(rng, extent, pieces, -0.22, 0.18) * entries
    return jnp.clip(entries, min=-most, max=most).astype(held_as)


def setup_inputs(seed: int = 0) -> dict:
    splits = jax.random.split(jax.random.key(seed), 8)
    tokens = centred(splits[0], (LENGTH, D), 1.0, 6.0, ((0, 4),))
    norm_gain = jnp.clip(1.0 + 0.18 * jax.random.normal(splits[1], (D,), jnp.float32), 0.1, 1.9)
    in_weight = centred(splits[2], (3, D, C), D ** -0.5, 0.0625, ((1, 4), (2, 8)))
    short_filter = centred(splits[3], (KS, 3, C), 0.4, 2.4, ((2, 8),), jnp.float32)
    long_filter = centred(splits[4], (KL, NF), (KL ** -0.5), 0.5, ((1, 8),), jnp.float32)
    out_weight = centred(splits[5], (C, D), C ** -0.5, 0.0625, ((0, 8), (1, 4)))
    segment_ids = jnp.searchsorted(jnp.cumsum(ragged(splits[6], SEGS, LENGTH, TOK_DEV, 1)), jnp.arange(LENGTH), side="right").astype(jnp.int32)
    return dict(tokens=tokens, norm_gain=norm_gain, in_weight=in_weight, short_filter=short_filter, long_filter=long_filter, out_weight=out_weight, segment_ids=segment_ids)


def reference(tokens, norm_gain, in_weight, short_filter, long_filter, out_weight, segment_ids):
    widened = tokens.astype(jnp.float32)
    squares = lax.optimization_barrier(jnp.mean(widened * widened, axis=1, keepdims=True))
    normed = (widened * lax.rsqrt(squares + 1e-06) * norm_gain).astype(jnp.bfloat16)
    projected = jnp.stack([jnp.dot(normed, in_weight[branch], preferred_element_type=jnp.float32) for branch in range(3)], axis=1).astype(jnp.bfloat16)
    seq_len = tokens.shape[0]
    ids_padded = jnp.concatenate([jnp.full((KL,), -1, jnp.int32), segment_ids.astype(jnp.int32)])
    proj_padded = jnp.concatenate([jnp.zeros((KL,) + projected.shape[1:], jnp.bfloat16), projected], axis=0)
    conv_short = jnp.zeros(projected.shape, jnp.float32)
    for offset in range(KS):
        source = proj_padded[KL - offset:KL - offset + seq_len].astype(jnp.float32)
        same_seg = (ids_padded[KL - offset:KL - offset + seq_len] == segment_ids).astype(jnp.float32)
        conv_short = conv_short + short_filter[offset][None] * source * same_seg[:, None, None]
    product = (conv_short[:, 1, :] * conv_short[:, 2, :]).astype(jnp.bfloat16)
    taps_chan = jnp.repeat(long_filter, GROUP, axis=1)
    prod_padded = jnp.concatenate([jnp.zeros((KL, product.shape[1]), jnp.bfloat16), product], axis=0)

    def add_tap(offset, running):
        begin = (KL - offset).astype(jnp.int32)
        source = lax.dynamic_slice_in_dim(prod_padded, begin, seq_len, 0).astype(jnp.float32)
        ids_here = lax.dynamic_slice_in_dim(ids_padded, begin, seq_len, 0)
        same_seg = (ids_here == segment_ids).astype(jnp.float32)
        tap_row = lax.dynamic_slice_in_dim(taps_chan, offset.astype(jnp.int32), 1, 0)
        return running + tap_row * source * same_seg[:, None]
    conv_long = lax.fori_loop(0, KL, add_tap, jnp.zeros(product.shape, jnp.float32))
    gated = (conv_short[:, 0, :] * conv_long).astype(jnp.bfloat16)
    mixed = jnp.dot(gated, out_weight, preferred_element_type=jnp.float32)
    return (widened + mixed).astype(jnp.bfloat16)
```

```python
import functools
import jax
import jax.numpy as jnp
from jax import lax
from jax.experimental import pallas as pl
from jax.experimental.pallas import tpu as pltpu
from jax.sharding import PartitionSpec as P

GROUP = 16
KS = 7
KL = 128
BF = jnp.bfloat16
F32 = jnp.float32
VMEM_MAX = 48 * 1024 * 1024


def in_proj_body(x_ref, w_ref, o_ref):
    pieces, rows = o_ref.shape[1], o_ref.shape[3]
    for i in range(pieces):
        acc = jnp.dot(x_ref[pl.ds(i * rows, rows), :], w_ref[0], preferred_element_type=F32)
        o_ref[0, i, 0] = acc.astype(BF)


def in_proj(x, w, parts):
    pieces, rows, depth = x.shape
    chan = w.shape[2]
    width = chan // parts
    if width % 128:
        y = jnp.einsum("ird,kdpc->pikrc", x, w.reshape(3, depth, parts, width), preferred_element_type=F32)
        return y.astype(BF)
    return pl.pallas_call(
        in_proj_body,
        grid=(parts, 3),
        in_specs=[
            pl.BlockSpec((pieces * rows, depth), lambda p, k: (0, 0)),
            pl.BlockSpec((1, depth, width), lambda p, k: (k, 0, p)),
        ],
        out_specs=pl.BlockSpec((1, pieces, 1, rows, width), lambda p, k: (p, 0, k, 0, 0)),
        out_shape=jax.ShapeDtypeStruct((parts, pieces, 3, rows, width), BF),
        compiler_params=pltpu.CompilerParams(vmem_limit_bytes=VMEM_MAX),
        cost_estimate=pl.CostEstimate(
            flops=2 * pieces * rows * depth * 3 * chan,
            bytes_accessed=2 * (3 * depth * chan + pieces * rows * (depth + 3 * chan)),
            transcendentals=0,
        ),
    )(x.reshape(pieces * rows, depth), w)


def conv_body(groups, shards, index_ref, y_ref, pos_ref, short_ref, taps_ref, o_ref, proj, prod, toep):
    pieces, rows = y_ref.shape[0], y_ref.shape[2]
    lanes = y_ref.shape[3]
    part = rows // shards
    seq_len = o_ref.shape[0]
    shard_len = seq_len // shards
    base = index_ref[0]
    for k in range(3):
        proj[k, pl.ds(0, 8), :] = jnp.zeros((8, lanes), F32)
        for q in range(pieces):
            piece = lax.bitwise_xor(jnp.int32(q), base)
            for t in range(shards):
                proj[k, pl.ds(8 + t * shard_len + q * part, part), :] = y_ref[
                    piece, k, pl.ds(t * part, part), :
                ].astype(F32)
    prod[pl.ds(0, KL), :] = jnp.zeros((KL, lanes), BF)
    for g in range(groups):
        row = jnp.broadcast_to(taps_ref[0, pl.ds(g, 1), :], (KL, 2 * KL))
        toep[pl.ds(g * KL, KL), :] = pltpu.roll(row, 0, 1, stride=1, stride_axis=0)
    lag = (
        KL
        + lax.broadcasted_iota(jnp.int32, (KL, 2 * KL), 0)
        - lax.broadcasted_iota(jnp.int32, (KL, 2 * KL), 1)
    )
    group_of = lax.broadcasted_iota(jnp.int32, (KL, lanes), 1) // GROUP

    def block(b, carry):
        start = pl.multiple_of(b * KL, KL)
        pos = pos_ref[pl.ds(start, KL), :]
        pos_lanes = jnp.broadcast_to(pos, (KL, lanes))
        sums = [None, None, None]
        window = [proj[k, pl.ds(start, KL + 8), :] for k in range(3)]
        for j in range(KS):
            keep = pos_lanes >= j
            for k in range(3):
                source = window[k][8 - j : 8 - j + KL]
                term = short_ref[j, k : k + 1, :] * source
                if j == 0:
                    sums[k] = term
                else:
                    sums[k] = sums[k] + jnp.where(keep, term, 0.0)
        prod[pl.ds(start + KL, KL), :] = (sums[1] * sums[2]).astype(BF)
        source = prod[pl.ds(start, 2 * KL), :]
        linked = (lag <= jnp.broadcast_to(pos, (KL, 2 * KL))) & (lag >= 0)
        total = jnp.zeros((KL, lanes), F32)
        for g in range(groups):
            masked = jnp.where(linked, toep[pl.ds(g * KL, KL), :], 0.0).astype(BF)
            made = jnp.dot(masked, source, preferred_element_type=F32)
            total = jnp.where(group_of == g, made, total)
        o_ref[pl.ds(start, KL), :] = (sums[0] * total).astype(BF)
        return carry

    lax.fori_loop(0, seq_len // KL, block, 0)


def convolve(y, position, short, taps, shards, base):
    pieces, _, rows, chan = y.shape
    seq_len = pieces * rows
    tile = 128 if chan % 128 == 0 else chan
    groups = tile // GROUP
    return pl.pallas_call(
        functools.partial(conv_body, groups, shards),
        grid_spec=pltpu.PrefetchScalarGridSpec(
            num_scalar_prefetch=1,
            grid=(chan // tile,),
            in_specs=[
                pl.BlockSpec((pieces, 3, rows, tile), lambda c, s: (0, 0, 0, c)),
                pl.BlockSpec((seq_len, 1), lambda c, s: (0, 0)),
                pl.BlockSpec((KS, 3, tile), lambda c, s: (0, 0, c)),
                pl.BlockSpec((1, groups, 2 * KL), lambda c, s: (c, 0, 0)),
            ],
            out_specs=pl.BlockSpec((seq_len, tile), lambda c, s: (0, c)),
            scratch_shapes=[
                pltpu.VMEM((3, seq_len + 8, tile), F32),
                pltpu.VMEM((seq_len + KL, tile), BF),
                pltpu.VMEM((groups * KL, 2 * KL), F32),
            ],
        ),
        out_shape=jax.ShapeDtypeStruct((seq_len, chan), BF),
        compiler_params=pltpu.CompilerParams(vmem_limit_bytes=VMEM_MAX),
        cost_estimate=pl.CostEstimate(
            flops=2 * seq_len * chan * 2 * KL * groups,
            bytes_accessed=seq_len * chan * 8,
            transcendentals=0,
        ),
    )(base, y, position, short, taps.reshape(chan // tile, groups, 2 * KL))


def out_proj_body(g_ref, w_ref, o_ref):
    parts, width = g_ref.shape[0], g_ref.shape[2]
    blocks, rows = o_ref.shape[0], o_ref.shape[2]
    for t in range(blocks):
        acc = None
        for p in range(parts):
            made = jnp.dot(
                g_ref[p, pl.ds(t * rows, rows), :],
                w_ref[pl.ds(p * width, width), :],
                preferred_element_type=F32,
            )
            acc = made if acc is None else acc + made
        o_ref[t, 0] = acc.astype(BF)


def out_proj(g, w, blocks, halves):
    parts, seq_len, width = g.shape
    depth = w.shape[1]
    cols = depth // halves
    tile = min(256, cols)
    per = cols // tile
    rows = seq_len // blocks
    return pl.pallas_call(
        out_proj_body,
        grid=(depth // tile,),
        in_specs=[
            pl.BlockSpec((parts, seq_len, width), lambda n: (0, 0, 0)),
            pl.BlockSpec((parts * width, tile), lambda n: (0, n)),
        ],
        out_specs=pl.BlockSpec((blocks, 1, rows, tile), lambda n: (0, n // per, 0, n % per)),
        out_shape=jax.ShapeDtypeStruct((blocks, halves, rows, cols), BF),
        compiler_params=pltpu.CompilerParams(vmem_limit_bytes=VMEM_MAX),
        cost_estimate=pl.CostEstimate(
            flops=2 * seq_len * parts * width * depth,
            bytes_accessed=2 * (parts * width * (seq_len + depth) + seq_len * depth),
            transcendentals=0,
        ),
    )(g, w)


def shards(tokens, norm_gain, in_weight, short_filter, long_filter, out_weight, segment_ids):
    n_seq, n_fsdp, n_tp = (lax.axis_size(a) for a in ("seq", "fsdp", "tp"))
    plane = n_fsdp * n_tp
    rows_dev, width_all = tokens.shape
    depth = in_weight.shape[1]
    chan_dev = in_weight.shape[2]
    z, f, c = (lax.axis_index(a) for a in ("seq", "fsdp", "tp"))
    q = f * n_tp + c
    rows = rows_dev // plane
    seq_len = segment_ids.shape[0]

    def swap_core(v):
        return lax.ppermute(v, "tp", [(i, i ^ 1) for i in range(n_tp)])

    def swap_chip(v, e):
        return lax.ppermute(v, "fsdp", [(i, i ^ e) for i in range(n_fsdp)])

    mine = lax.dynamic_slice_in_dim(tokens, q * rows, rows, 0).astype(F32)
    squares = jnp.mean(mine * mine, axis=1, keepdims=True)
    normed = (mine * lax.rsqrt(squares + 1e-06) * norm_gain).astype(BF)
    split = normed.reshape(rows, n_seq, depth).transpose(1, 0, 2)
    own = lax.all_to_all(split, "seq", 0, 0).reshape(n_seq * rows, depth)
    near = swap_core(own)
    far = [swap_chip(own, e) for e in range(1, n_fsdp)]
    first = in_proj(jnp.stack([own, near]), in_weight, n_seq)
    got_first = lax.psum_scatter(first, "seq", scatter_dimension=0)
    far_pairs = []
    for e in range(n_fsdp - 1):
        far_pairs += [far[e], swap_core(far[e])]
    second = in_proj(jnp.stack(far_pairs), in_weight, n_seq)
    got_second = lax.psum_scatter(second, "seq", scatter_dimension=0)
    projected = jnp.concatenate([got_first, got_second], axis=0)

    chan = chan_dev // n_seq
    groups = chan // GROUP
    at = jnp.arange(seq_len, dtype=jnp.int32)
    earlier = (segment_ids[None, :] == segment_ids[:, None]) & (at[None, :] < at[:, None])
    position = jnp.sum(earlier.astype(jnp.int32), axis=1, keepdims=True)
    short = lax.dynamic_slice_in_dim(short_filter, z * chan, chan, 2)
    taps = lax.dynamic_slice_in_dim(long_filter, z * groups, groups, 1)
    taps = jnp.concatenate(
        [jnp.zeros((1, groups), F32), taps[::-1], jnp.zeros((KL - 1, groups), F32)], axis=0
    ).T
    gated = convolve(projected, position, short, taps, n_seq, q.astype(jnp.int32).reshape(1))

    gathered = lax.all_gather(gated, "seq", axis=0)
    halves = plane // n_seq
    partial = out_proj(gathered, out_weight, n_seq, halves)
    cols = partial.shape[3]
    partial = partial.reshape(n_fsdp, n_tp, rows_dev, cols)
    away = lax.dynamic_index_in_dim(partial, 1 - c, 1, keepdims=False)
    keep = lax.dynamic_index_in_dim(partial, c, 1, keepdims=False)
    both = (keep.astype(F32) + swap_core(away).astype(F32)).astype(BF)
    total = lax.dynamic_index_in_dim(both, f, 0, keepdims=False).astype(F32)
    for e in range(1, n_fsdp):
        sent = lax.dynamic_index_in_dim(both, f ^ e, 0, keepdims=False)
        total = total + swap_chip(sent, e).astype(F32)
    total = total.astype(BF)

    def flat(s, p):
        return (p // n_tp * n_seq + s) * n_tp + p % n_tp

    pairs = [
        (flat(s, p), flat(p // halves, s * halves + p % halves))
        for s in range(n_seq)
        for p in range(plane)
    ]
    placed = lax.ppermute(total, ("fsdp", "seq", "tp"), pairs)
    residual = lax.dynamic_slice_in_dim(tokens, q * cols, cols, 1)
    return (residual.astype(F32) + placed.astype(F32)).astype(BF)


def solution(mesh):
    return jax.shard_map(
        shards,
        mesh=mesh,
        in_specs=(
            P("seq", None),
            P(),
            P(None, "seq", ("fsdp", "tp")),
            P(None, None, ("fsdp", "tp")),
            P(None, ("fsdp", "tp")),
            P(("fsdp", "tp"), "seq"),
            P(),
        ),
        out_specs=P("seq", ("fsdp", "tp")),
        check_vma=False,
    )
```

```python
import functools
import jax
import jax.numpy as jnp
from jax import lax
from jax.experimental import pallas as pl
from jax.experimental.pallas import tpu as pltpu
from jax.sharding import PartitionSpec as P

GROUP = 16
SPLIT = 128
KS = 7
KL = 128
BF = jnp.bfloat16
F32 = jnp.float32
MIB = 1024 * 1024


def in_proj_body(x_ref, w_ref, o_ref):
    parts, pieces, rows, width = o_ref.shape[0], o_ref.shape[1], o_ref.shape[3], o_ref.shape[4]
    made = jnp.dot(x_ref[...], w_ref[0], preferred_element_type=F32).astype(BF)
    for p in range(parts):
        for i in range(pieces):
            o_ref[p, i, 0] = made[i * rows : (i + 1) * rows, p * width : (p + 1) * width]


def in_proj(x, w, parts, weight=1):
    pieces, rows, depth = x.shape
    chan = w.shape[2]
    width = chan // parts
    if width % 128:
        y = jnp.einsum("ird,kdpc->pikrc", x, w.reshape(3, depth, parts, width), preferred_element_type=F32)
        return y.astype(BF)
    tile = chan if pieces * rows <= 256 else max(width, chan // 2)
    each = tile // width
    return pl.pallas_call(
        in_proj_body,
        grid=(3, chan // tile),
        in_specs=[
            pl.BlockSpec((pieces * rows, depth), lambda k, p: (0, 0)),
            pl.BlockSpec((1, depth, tile), lambda k, p: (k, 0, p)),
        ],
        out_specs=pl.BlockSpec((each, pieces, 1, rows, width), lambda k, p: (p, 0, k, 0, 0)),
        out_shape=jax.ShapeDtypeStruct((parts, pieces, 3, rows, width), BF),
        compiler_params=pltpu.CompilerParams(vmem_limit_bytes=48 * MIB),
        cost_estimate=pl.CostEstimate(
            flops=2 * pieces * rows * depth * 3 * chan * weight,
            bytes_accessed=2 * (3 * depth * chan + pieces * rows * (depth + 3 * chan)),
            transcendentals=0,
        ),
    )(x.reshape(pieces * rows, depth), w)


def conv_body(groups, base_ref, a_ref, b_ref, pos_ref, short_ref, taps_ref, *refs):
    outs, (proj, prod, toep) = refs[:-3], refs[-3:]
    shards = outs[0].shape[0]
    rows, lanes = a_ref.shape[2], a_ref.shape[3]
    part = rows // shards
    shard_len = sum(o.shape[1] for o in outs)
    near = a_ref.shape[0]
    for k in range(3):
        proj[k, pl.ds(0, 8), :] = jnp.zeros((8, lanes), F32)
    for i in range(near + b_ref.shape[0]):
        y_ref, at, base = (a_ref, i, base_ref[0]) if i < near else (b_ref, i - near, base_ref[1])
        offset = lax.bitwise_xor(jnp.int32(i), base) * part + 8
        for t in range(shards):
            place = pl.ds(pl.multiple_of(offset + t * shard_len, 8), part)
            for k in range(3):
                proj[k, place, :] = y_ref[at, k, pl.ds(t * part, part), :].astype(F32)
    prod[pl.ds(0, KL), :] = jnp.zeros((KL, lanes), BF)
    for g in range(groups):
        row = jnp.broadcast_to(taps_ref[0, pl.ds(g, 1), :], (KL, 2 * KL))
        toep[pl.ds(g * KL, KL), :] = pltpu.roll(row, 0, 1, stride=1, stride_axis=0)
    lag = (
        KL
        + lax.broadcasted_iota(jnp.int32, (KL, 2 * KL), 0)
        - lax.broadcasted_iota(jnp.int32, (KL, 2 * KL), 1)
    )
    group_of = lax.broadcasted_iota(jnp.int32, (KL, lanes), 1) // GROUP

    def block(start):
        pos = pos_ref[pl.ds(start, KL), :]
        pos_lanes = jnp.broadcast_to(pos, (KL, lanes))
        sums = [None, None, None]
        window = [proj[k, pl.ds(start, KL + 8), :] for k in range(3)]
        for j in range(KS):
            keep = pos_lanes >= j
            for k in range(3):
                source = window[k][8 - j : 8 - j + KL]
                term = short_ref[j, k : k + 1, :] * source
                if j == 0:
                    sums[k] = term
                else:
                    sums[k] = sums[k] + jnp.where(keep, term, 0.0)
        prod[pl.ds(start + KL, KL), :] = (sums[1] * sums[2]).astype(BF)
        source = prod[pl.ds(start, 2 * KL), :]
        linked = (lag <= jnp.broadcast_to(pos, (KL, 2 * KL))) & (lag >= 0)
        total = jnp.zeros((KL, lanes), F32)
        for g in range(groups):
            masked = jnp.where(linked, toep[pl.ds(g * KL, KL), :], 0.0).astype(BF)
            made = jnp.dot(masked, source, preferred_element_type=F32)
            total = jnp.where(group_of == g, made, total)
        return (sums[0] * total).astype(BF)

    def shard(t, carry):
        for b in range(shard_len // KL):
            gated = block(pl.multiple_of(t * shard_len + b * KL, KL))
            begin = 0
            for o in outs:
                end = begin + o.shape[1]
                lo, hi = max(begin, b * KL), min(end, b * KL + KL)
                if lo < hi:
                    o[t, lo - begin : hi - begin, :] = gated[lo - b * KL : hi - b * KL]
                begin = end
        return carry

    lax.fori_loop(0, shards, shard, 0)


def convolve(first, second, position, short, taps, shards, base, splits):
    pieces, _, rows, chan = second.shape
    near = first.shape[0]
    pieces += near
    seq_len = pieces * rows
    tile = 128 if chan % 128 == 0 else chan
    groups = tile // GROUP
    return pl.pallas_call(
        functools.partial(conv_body, groups),
        grid_spec=pltpu.PrefetchScalarGridSpec(
            num_scalar_prefetch=1,
            grid=(chan // tile,),
            in_specs=[
                pl.BlockSpec((near, 3, rows, tile), lambda c, s: (0, 0, 0, c)),
                pl.BlockSpec((pieces - near, 3, rows, tile), lambda c, s: (0, 0, 0, c)),
                pl.BlockSpec((seq_len, 1), lambda c, s: (0, 0)),
                pl.BlockSpec((KS, 3, tile), lambda c, s: (0, 0, c)),
                pl.BlockSpec((1, groups, 2 * KL), lambda c, s: (c, 0, 0)),
            ],
            out_specs=[pl.BlockSpec((shards, n, tile), lambda c, s: (0, 0, c)) for n in splits],
            scratch_shapes=[
                pltpu.VMEM((3, seq_len + 8, tile), F32),
                pltpu.VMEM((seq_len + KL, tile), BF),
                pltpu.VMEM((groups * KL, 2 * KL), F32),
            ],
        ),
        out_shape=[jax.ShapeDtypeStruct((shards, n, chan), BF) for n in splits],
        compiler_params=pltpu.CompilerParams(vmem_limit_bytes=48 * MIB),
        cost_estimate=pl.CostEstimate(
            flops=2 * seq_len * chan * 2 * KL * groups,
            bytes_accessed=seq_len * chan * 8,
            transcendentals=0,
        ),
    )(base, first, second, position, short, taps.reshape(chan // tile, groups, 2 * KL))


def out_proj_body(place_ref, g_ref, w_ref, o_ref):
    parts, seq_len = g_ref.shape[0], g_ref.shape[1]
    pieces, rows = o_ref.shape[0], o_ref.shape[1]

    def product(at):
        left = jnp.concatenate([g_ref[p, at, :] for p in range(parts)], axis=1)
        return jnp.dot(left, w_ref[...], preferred_element_type=F32).astype(BF)

    if pieces * rows == seq_len:
        made = product(pl.ds(0, seq_len))
        for t in range(pieces):
            o_ref[place_ref[1 + pieces + t]] = made[t * rows : (t + 1) * rows]
    else:
        for e in range(pieces):
            at = pl.multiple_of(place_ref[1 + e] * rows, rows)
            o_ref[e] = product(pl.ds(at, rows))


def out_proj(g, w, place, pieces, rows, cols):
    parts, seq_len, width = g.shape
    tile = min(512, cols)
    per = cols // tile
    return pl.pallas_call(
        out_proj_body,
        grid_spec=pltpu.PrefetchScalarGridSpec(
            num_scalar_prefetch=1,
            grid=(per,),
            in_specs=[
                pl.BlockSpec((parts, seq_len, width), lambda n, s: (0, 0, 0)),
                pl.BlockSpec((parts * width, tile), lambda n, s: (0, s[0] * per + n)),
            ],
            out_specs=pl.BlockSpec((pieces, rows, tile), lambda n, s: (0, 0, n)),
        ),
        out_shape=jax.ShapeDtypeStruct((pieces, rows, cols), BF),
        compiler_params=pltpu.CompilerParams(vmem_limit_bytes=48 * MIB),
        cost_estimate=pl.CostEstimate(
            flops=2 * pieces * rows * parts * width * cols * 16,
            bytes_accessed=2 * (parts * width * (seq_len + cols) + pieces * rows * cols),
            transcendentals=0,
        ),
    )(place, g, w)


def shards(tokens, norm_gain, in_weight, short_filter, long_filter, out_weight, segment_ids):
    n_seq, n_fsdp, n_tp = (lax.axis_size(a) for a in ("seq", "fsdp", "tp"))
    plane = n_fsdp * n_tp
    rows_dev, width_all = tokens.shape
    depth = in_weight.shape[1]
    chan_dev = in_weight.shape[2]
    z, f, c = (lax.axis_index(a) for a in ("seq", "fsdp", "tp"))
    q = f * n_tp + c
    rows = rows_dev // plane
    seq_len = segment_ids.shape[0]

    def swap_core(v):
        return lax.ppermute(v, "tp", [(i, i ^ 1) for i in range(n_tp)])

    def swap_chip(v, e):
        return lax.ppermute(v, "fsdp", [(i, i ^ e) for i in range(n_fsdp)])

    mine = lax.dynamic_slice_in_dim(tokens, q * rows, rows, 0).astype(F32)
    squares = jnp.mean(mine * mine, axis=1, keepdims=True)
    normed = (mine * lax.rsqrt(squares + 1e-06) * norm_gain).astype(BF)
    split = normed.reshape(rows, n_seq, depth).transpose(1, 0, 2)
    own = lax.all_to_all(split, "seq", 0, 0).reshape(n_seq * rows, depth)
    near = swap_core(own)
    far = [swap_chip(own, e) for e in range(1, n_fsdp)]
    first = in_proj(jnp.stack([own, near]), in_weight, n_seq)
    got_first = lax.psum_scatter(first, "seq", scatter_dimension=0)
    far, first = lax.optimization_barrier((far, first))
    both = jnp.broadcast_to(jnp.stack(far)[None], (n_tp, n_fsdp - 1, n_seq * rows, depth))
    both = lax.all_to_all(both, "tp", 0, 0)
    both = both.transpose(1, 0, 2, 3).reshape(n_tp * (n_fsdp - 1), n_seq * rows, depth)
    second = in_proj(both, in_weight, n_seq, 10)
    got_second = lax.psum_scatter(second, "seq", scatter_dimension=0)

    chan = chan_dev // n_seq
    groups = chan // GROUP
    at = jnp.arange(seq_len, dtype=jnp.int32)
    earlier = (segment_ids[None, :] == segment_ids[:, None]) & (at[None, :] < at[:, None])
    position = jnp.sum(earlier.astype(jnp.int32), axis=1, keepdims=True)
    short = lax.dynamic_slice_in_dim(short_filter, z * chan, chan, 2)
    taps = lax.dynamic_slice_in_dim(long_filter, z * groups, groups, 1)
    taps = jnp.concatenate(
        [jnp.zeros((1, groups), F32), taps[::-1], jnp.zeros((KL - 1, groups), F32)], axis=0
    ).T
    splits = (SPLIT, rows_dev - SPLIT)
    base = jnp.stack([q, f * n_tp]).astype(jnp.int32)
    gated = convolve(got_first, got_second, position, short, taps, n_seq, base, splits)

    halves = plane // n_seq
    cols = out_weight.shape[1] // halves

    def block_of(p):
        return lax.bitwise_xor(p // halves, z)

    def place_for(core):
        piece = [lax.bitwise_xor(f, e) * n_tp + core for e in range(n_fsdp)]
        blocks = [block_of(p) for p in piece]
        inverse = [lax.bitwise_xor(lax.bitwise_xor(t, z) * halves // n_tp, f) for t in range(n_fsdp)]
        return jnp.stack([piece[0] % halves] + blocks + inverse).astype(jnp.int32)

    place_away, place_keep = place_for(1 - c), place_for(c)

    def flat(s, p):
        return (p // n_tp * n_seq + s) * n_tp + p % n_tp

    pairs = [
        (flat(s, p), flat((p // halves) ^ s, s * halves + p % halves))
        for s in range(n_seq)
        for p in range(plane)
    ]
    placed, sends = [], None
    gathers = [lax.all_gather(part, "seq", axis=0) for part in gated]
    for gathered, count in zip(gathers, splits):
        if sends is not None:
            gathered, sends = lax.optimization_barrier((gathered, sends))
            placed[-1] = sends
        gathered = gathered.reshape(n_seq, n_seq * count, chan)
        away = out_proj(gathered, out_weight, place_away, n_fsdp, count, cols)
        near = swap_core(away)
        keep = out_proj(gathered, out_weight, place_keep, n_fsdp, count, cols)
        total = keep[0].astype(F32) + near[0].astype(F32)
        sends = [(keep[e].astype(F32) + near[e].astype(F32)).astype(BF) for e in range(1, n_fsdp)]
        for e in range(1, n_fsdp):
            total = total + swap_chip(sends[e - 1], e).astype(F32)
        sends = total.astype(BF)
        placed.append(sends)
    placed = [lax.ppermute(p, ("fsdp", "seq", "tp"), pairs) for p in placed]
    residual = lax.dynamic_slice_in_dim(tokens, q * cols, cols, 1)
    return (residual.astype(F32) + jnp.concatenate(placed, axis=0).astype(F32)).astype(BF)


def solution(mesh):
    return jax.shard_map(
        shards,
        mesh=mesh,
        in_specs=(
            P("seq", None),
            P(),
            P(None, "seq", ("fsdp", "tp")),
            P(None, None, ("fsdp", "tp")),
            P(None, ("fsdp", "tp")),
            P(("fsdp", "tp"), "seq"),
            P(),
        ),
        out_specs=P("seq", ("fsdp", "tp")),
        check_vma=False,
    )
```

```python
import functools
import jax
import jax.numpy as jnp
from jax import lax
from jax.experimental import pallas as pl
from jax.experimental.pallas import tpu as pltpu
from jax.sharding import PartitionSpec as P

GROUP = 16
SPLIT = 160
KS = 7
KL = 128
BF = jnp.bfloat16
F32 = jnp.float32
MIB = 1024 * 1024


def norm_body(at_ref, t_ref, gain_ref, o_ref):
    wide = t_ref[...].astype(F32)
    squares = jnp.mean(wide * wide, axis=1, keepdims=True)
    normed = (wide * lax.rsqrt(squares + 1e-06) * gain_ref[...]).astype(BF)
    parts, _, depth = o_ref.shape
    for p in range(parts):
        o_ref[p] = normed[:, p * depth : (p + 1) * depth]


def norm(tokens, gain, at, rows, parts):
    width = tokens.shape[1]
    return pl.pallas_call(
        norm_body,
        grid_spec=pltpu.PrefetchScalarGridSpec(
            num_scalar_prefetch=1,
            grid=(1,),
            in_specs=[
                pl.BlockSpec((rows, width), lambda i, s: (s[0], 0)),
                pl.BlockSpec((1, width), lambda i, s: (0, 0)),
            ],
            out_specs=pl.BlockSpec((parts, rows, width // parts), lambda i, s: (0, 0, 0)),
        ),
        out_shape=jax.ShapeDtypeStruct((parts, rows, width // parts), BF),
        compiler_params=pltpu.CompilerParams(vmem_limit_bytes=62 * MIB),
    )(at, tokens, gain.reshape(1, width))


def in_proj_body(x_ref, w_ref, o_ref):
    parts, pieces, rows, width = o_ref.shape[0], o_ref.shape[1], o_ref.shape[3], o_ref.shape[4]
    made = jnp.dot(x_ref[...], w_ref[0], preferred_element_type=F32).astype(BF)
    for p in range(parts):
        for i in range(pieces):
            o_ref[p, i, 0] = made[i * rows : (i + 1) * rows, p * width : (p + 1) * width]


def in_proj(x, w, parts, weight=1):
    pieces, rows, depth = x.shape
    chan = w.shape[2]
    width = chan // parts
    if width % 128:
        y = jnp.einsum("ird,kdpc->pikrc", x, w.reshape(3, depth, parts, width), preferred_element_type=F32)
        return y.astype(BF)
    tile = chan if pieces * rows <= 256 else max(width, chan // 2)
    each = tile // width
    return pl.pallas_call(
        in_proj_body,
        grid=(3, chan // tile),
        in_specs=[
            pl.BlockSpec((pieces * rows, depth), lambda k, p: (0, 0)),
            pl.BlockSpec((1, depth, tile), lambda k, p: (k, 0, p)),
        ],
        out_specs=pl.BlockSpec((each, pieces, 1, rows, width), lambda k, p: (p, 0, k, 0, 0)),
        out_shape=jax.ShapeDtypeStruct((parts, pieces, 3, rows, width), BF),
        compiler_params=pltpu.CompilerParams(vmem_limit_bytes=48 * MIB),
        cost_estimate=pl.CostEstimate(
            flops=2 * pieces * rows * depth * 3 * chan * weight,
            bytes_accessed=2 * (3 * depth * chan + pieces * rows * (depth + 3 * chan)),
            transcendentals=0,
        ),
    )(x.reshape(pieces * rows, depth), w)


def toeplitz_body(taps_ref, o_ref):
    groups = taps_ref.shape[1]
    for g in range(groups):
        row = jnp.broadcast_to(taps_ref[0, pl.ds(g, 1), :], (KL, 2 * KL))
        o_ref[0, pl.ds(g * KL, KL), :] = pltpu.roll(row, 0, 1, stride=1, stride_axis=0).astype(BF)


def toeplitz(taps):
    tiles, groups, _ = taps.shape
    return pl.pallas_call(
        toeplitz_body,
        grid=(tiles,),
        in_specs=[pl.BlockSpec((1, groups, 2 * KL), lambda c: (c, 0, 0))],
        out_specs=pl.BlockSpec((1, groups * KL, 2 * KL), lambda c: (c, 0, 0)),
        out_shape=jax.ShapeDtypeStruct((tiles, groups * KL, 2 * KL), BF),
        cost_estimate=pl.CostEstimate(flops=0, bytes_accessed=0, transcendentals=0),
    )(taps)


def conv_body(groups, base_ref, a_ref, b_ref, pos_ref, short_ref, toep_ref, *refs):
    outs, (proj, prod) = refs[:-2], refs[-2:]
    shards = outs[0].shape[0]
    rows, lanes = a_ref.shape[2], a_ref.shape[3]
    part = rows // shards
    shard_len = sum(o.shape[1] for o in outs)
    near = a_ref.shape[0]
    for k in range(3):
        proj[k, pl.ds(0, 8), :] = jnp.zeros((8, lanes), F32)
    for i in range(near + b_ref.shape[0]):
        y_ref, at = (a_ref, i) if i < near else (b_ref, i - near)
        others = b_ref.shape[0] // near
        apart = i if i < near else (1 + at % others) * near + at // others
        offset = lax.bitwise_xor(jnp.int32(apart), base_ref[0]) * part + 8
        for t in range(shards):
            place = pl.ds(pl.multiple_of(offset + t * shard_len, 8), part)
            for k in range(3):
                proj[k, place, :] = y_ref[at, k, pl.ds(t * part, part), :].astype(F32)
    prod[pl.ds(0, KL), :] = jnp.zeros((KL, lanes), BF)
    lag = (
        KL
        + lax.broadcasted_iota(jnp.int32, (KL, 2 * KL), 0)
        - lax.broadcasted_iota(jnp.int32, (KL, 2 * KL), 1)
    )
    group_of = lax.broadcasted_iota(jnp.int32, (KL, lanes), 1) // GROUP

    def block(start):
        pos = pos_ref[pl.ds(start, KL), :]
        pos_lanes = jnp.broadcast_to(pos, (KL, lanes))
        sums = [None, None, None]
        for j in range(KS):
            keep = pos_lanes >= j
            for k in range(3):
                source = proj[k, pl.ds(start + (8 - j), KL), :]
                term = short_ref[j, k : k + 1, :] * source
                if j == 0:
                    sums[k] = term
                else:
                    sums[k] = sums[k] + jnp.where(keep, term, 0.0)
        prod[pl.ds(start + KL, KL), :] = (sums[1] * sums[2]).astype(BF)
        source = prod[pl.ds(start, 2 * KL), :]
        linked = (lag <= jnp.broadcast_to(pos, (KL, 2 * KL))) & (lag >= 0)
        linked = linked.astype(F32).astype(BF)
        total = jnp.zeros((KL, lanes), F32)
        for g in range(groups):
            masked = toep_ref[0, pl.ds(g * KL, KL), :] * linked
            made = jnp.dot(masked, source, preferred_element_type=F32)
            total = jnp.where(group_of == g, made, total)
        return (sums[0] * total).astype(BF)

    def shard(t, carry):
        for b in range(shard_len // KL):
            gated = block(pl.multiple_of(t * shard_len + b * KL, KL))
            begin = 0
            for o in outs:
                end = begin + o.shape[1]
                lo, hi = max(begin, b * KL), min(end, b * KL + KL)
                if lo < hi:
                    o[t, lo - begin : hi - begin, :] = gated[lo - b * KL : hi - b * KL]
                begin = end
        return carry

    lax.fori_loop(0, shards, shard, 0)


def convolve(first, second, position, short, matrices, shards, base, splits):
    pieces, _, rows, chan = second.shape
    near = first.shape[0]
    pieces += near
    seq_len = pieces * rows
    tile = chan // matrices.shape[0]
    groups = tile // GROUP
    return pl.pallas_call(
        functools.partial(conv_body, groups),
        grid_spec=pltpu.PrefetchScalarGridSpec(
            num_scalar_prefetch=1,
            grid=(chan // tile,),
            in_specs=[
                pl.BlockSpec((near, 3, rows, tile), lambda c, s: (0, 0, 0, c)),
                pl.BlockSpec((pieces - near, 3, rows, tile), lambda c, s: (0, 0, 0, c)),
                pl.BlockSpec((seq_len, 1), lambda c, s: (0, 0)),
                pl.BlockSpec((KS, 3, tile), lambda c, s: (0, 0, c)),
                pl.BlockSpec((1, groups * KL, 2 * KL), lambda c, s: (c, 0, 0)),
            ],
            out_specs=[pl.BlockSpec((shards, n, tile), lambda c, s: (0, 0, c)) for n in splits],
            scratch_shapes=[
                pltpu.VMEM((3, seq_len + 8, tile), F32),
                pltpu.VMEM((seq_len + KL, tile), BF),
            ],
        ),
        out_shape=[jax.ShapeDtypeStruct((shards, n, chan), BF) for n in splits],
        compiler_params=pltpu.CompilerParams(vmem_limit_bytes=62 * MIB),
        cost_estimate=pl.CostEstimate(
            flops=2 * seq_len * chan * 2 * KL * groups,
            bytes_accessed=seq_len * chan * 8,
            transcendentals=0,
        ),
    )(base, first, second, position, short, matrices)


def out_proj_body(place_ref, g_ref, w_ref, o_ref):
    parts, seq_len = g_ref.shape[0], g_ref.shape[1]
    pieces, rows = o_ref.shape[0], o_ref.shape[1]

    def product(at):
        left = jnp.concatenate([g_ref[p, at, :] for p in range(parts)], axis=1)
        return jnp.dot(left, w_ref[...], preferred_element_type=F32).astype(BF)

    if pieces * rows == seq_len:
        made = product(pl.ds(0, seq_len))
        for t in range(pieces):
            o_ref[place_ref[1 + pieces + t]] = made[t * rows : (t + 1) * rows]
    else:
        for e in range(pieces):
            at = pl.multiple_of(place_ref[1 + e] * rows, rows)
            o_ref[e] = product(pl.ds(at, rows))


def out_proj(g, w, place, pieces, rows, cols):
    parts, seq_len, width = g.shape
    tile = min(512, cols)
    per = cols // tile
    return pl.pallas_call(
        out_proj_body,
        grid_spec=pltpu.PrefetchScalarGridSpec(
            num_scalar_prefetch=1,
            grid=(per,),
            in_specs=[
                pl.BlockSpec((parts, seq_len, width), lambda n, s: (0, 0, 0)),
                pl.BlockSpec((parts * width, tile), lambda n, s: (0, s[0] * per + n)),
            ],
            out_specs=pl.BlockSpec((pieces, rows, tile), lambda n, s: (0, 0, n)),
        ),
        out_shape=jax.ShapeDtypeStruct((pieces, rows, cols), BF),
        compiler_params=pltpu.CompilerParams(vmem_limit_bytes=48 * MIB),
        cost_estimate=pl.CostEstimate(
            flops=2 * pieces * rows * parts * width * cols * 16,
            bytes_accessed=2 * (parts * width * (seq_len + cols) + pieces * rows * cols),
            transcendentals=0,
        ),
    )(place, g, w)


def shards(tokens, norm_gain, in_weight, short_filter, long_filter, out_weight, segment_ids):
    n_seq, n_fsdp, n_tp = (lax.axis_size(a) for a in ("seq", "fsdp", "tp"))
    plane = n_fsdp * n_tp
    rows_dev, width_all = tokens.shape
    depth = in_weight.shape[1]
    chan_dev = in_weight.shape[2]
    z, f, c = (lax.axis_index(a) for a in ("seq", "fsdp", "tp"))
    q = f * n_tp + c
    rows = rows_dev // plane
    seq_len = segment_ids.shape[0]

    def swap_core(v):
        return lax.ppermute(v, "tp", [(i, i ^ 1) for i in range(n_tp)])

    def swap_chip(v, e):
        return lax.ppermute(v, "fsdp", [(i, i ^ e) for i in range(n_fsdp)])

    chan = chan_dev // n_seq
    groups = chan // GROUP
    taps = lax.dynamic_slice_in_dim(long_filter, z * groups, groups, 1)
    taps = jnp.concatenate(
        [jnp.zeros((1, groups), F32), taps[::-1], jnp.zeros((KL - 1, groups), F32)], axis=0
    ).T
    tiles = chan // 128 if chan % 128 == 0 else 1
    matrices = toeplitz(taps.reshape(tiles, groups // tiles, 2 * KL))
    split = norm(tokens, norm_gain, q.astype(jnp.int32).reshape(1), rows, n_seq)
    own = lax.all_to_all(split, "seq", 0, 0).reshape(n_seq * rows, depth)
    near = swap_core(own)
    far = [swap_chip(own, e) for e in range(1, n_fsdp)]
    first = in_proj(jnp.stack([own, near]), in_weight, n_seq)
    got_first = lax.psum_scatter(first, "seq", scatter_dimension=0)
    far, first = lax.optimization_barrier((far, first))
    far = jnp.stack(far)
    both = jnp.concatenate([far, swap_core(far)])
    both, matrices = lax.optimization_barrier((both, matrices))
    second = in_proj(both, in_weight, n_seq, 1)
    got_second = lax.psum_scatter(second, "seq", scatter_dimension=0)

    at = jnp.arange(seq_len, dtype=jnp.int32)
    earlier = (segment_ids[None, :] == segment_ids[:, None]) & (at[None, :] < at[:, None])
    position = jnp.sum(earlier.astype(jnp.int32), axis=1, keepdims=True)
    short = lax.dynamic_slice_in_dim(short_filter, z * chan, chan, 2)
    splits = (SPLIT, rows_dev - SPLIT)
    base = q.astype(jnp.int32).reshape(1)
    gated = convolve(got_first, got_second, position, short, matrices, n_seq, base, splits)

    halves = plane // n_seq
    cols = out_weight.shape[1] // halves

    def block_of(p):
        return lax.bitwise_xor(p // halves, z)

    def place_for(core):
        piece = [lax.bitwise_xor(f, e) * n_tp + core for e in range(n_fsdp)]
        blocks = [block_of(p) for p in piece]
        inverse = [lax.bitwise_xor(lax.bitwise_xor(t, z) * halves // n_tp, f) for t in range(n_fsdp)]
        return jnp.stack([piece[0] % halves] + blocks + inverse).astype(jnp.int32)

    place_away, place_keep = place_for(1 - c), place_for(c)

    def flat(s, p):
        return (p // n_tp * n_seq + s) * n_tp + p % n_tp

    pairs = [
        (flat(s, p), flat((p // halves) ^ s, s * halves + p % halves))
        for s in range(n_seq)
        for p in range(plane)
    ]
    placed, sends = [], None
    gathers = [lax.all_gather(part, "seq", axis=0) for part in gated]
    for gathered, count in zip(gathers, splits):
        if sends is not None:
            gathered, sends = lax.optimization_barrier((gathered, sends))
            placed[-1] = sends
        gathered = gathered.reshape(n_seq, n_seq * count, chan)
        away = out_proj(gathered, out_weight, place_away, n_fsdp, count, cols)
        near = swap_core(away)
        keep = out_proj(gathered, out_weight, place_keep, n_fsdp, count, cols)
        total = keep[0].astype(F32) + near[0].astype(F32)
        sends = [(keep[e].astype(F32) + near[e].astype(F32)).astype(BF) for e in range(1, n_fsdp)]
        for e in range(1, n_fsdp):
            total = total + swap_chip(sends[e - 1], e).astype(F32)
        sends = total.astype(BF)
        placed.append(sends)
    placed = [lax.ppermute(p, ("fsdp", "seq", "tp"), pairs) for p in placed]
    residual = lax.optimization_barrier(lax.dynamic_slice_in_dim(tokens, q * cols, cols, 1))
    return (residual.astype(F32) + jnp.concatenate(placed, axis=0).astype(F32)).astype(BF)


def solution(mesh):
    return jax.shard_map(
        shards,
        mesh=mesh,
        in_specs=(
            P("seq", None),
            P(),
            P(None, "seq", ("fsdp", "tp")),
            P(None, None, ("fsdp", "tp")),
            P(None, ("fsdp", "tp")),
            P(("fsdp", "tp"), "seq"),
            P(),
        ),
        out_specs=P("seq", ("fsdp", "tp")),
        check_vma=False,
    )
```

```python
import functools
import jax
import jax.numpy as jnp
from jax import lax
from jax.experimental import pallas as pl
from jax.experimental.pallas import tpu as pltpu
from jax.sharding import PartitionSpec as P

GROUP = 16
SPLIT = 80
KS = 7
KL = 128
BF = jnp.bfloat16
F32 = jnp.float32
MIB = 1024 * 1024


def norm_body(at_ref, t_ref, gain_ref, *refs):
    outs, held = refs[:-1], refs[-1]
    wide = t_ref[...].astype(F32)
    squares = jnp.mean(wide * wide, axis=1, keepdims=True)
    normed = (wide * lax.rsqrt(squares + 1e-06) * gain_ref[...]).astype(BF)
    depth = held.shape[2]
    for p in range(held.shape[0]):
        held[p] = normed[:, p * depth : (p + 1) * depth]
    for e, o in enumerate(outs):
        o[...] = held[lax.bitwise_xor(at_ref[1], e)]


def norm(tokens, gain, at, rows, parts):
    width = tokens.shape[1]
    depth = width // parts
    return pl.pallas_call(
        norm_body,
        grid_spec=pltpu.PrefetchScalarGridSpec(
            num_scalar_prefetch=1,
            grid=(1,),
            in_specs=[
                pl.BlockSpec((rows, width), lambda i, s: (s[0], 0)),
                pl.BlockSpec((1, width), lambda i, s: (0, 0)),
            ],
            out_specs=[pl.BlockSpec((rows, depth), lambda i, s: (0, 0))] * parts,
            scratch_shapes=[pltpu.VMEM((parts, rows, depth), BF)],
        ),
        out_shape=[jax.ShapeDtypeStruct((rows, depth), BF)] * parts,
        compiler_params=pltpu.CompilerParams(vmem_limit_bytes=62 * MIB),
    )(at, tokens, gain.reshape(1, width))


def in_proj_body(at_ref, x_ref, w_ref, o_ref, *, parts):
    each, pieces, rows, width = o_ref.shape[0], o_ref.shape[1], o_ref.shape[3], o_ref.shape[4]
    made = jnp.dot(x_ref[...], w_ref[0], preferred_element_type=F32).astype(BF)
    part = rows // parts
    for e in range(parts):
        place = pl.ds(pl.multiple_of(lax.bitwise_xor(at_ref[0], e) * part, part), part)
        for i in range(pieces):
            begin = i * rows + e * part
            for p in range(each):
                o_ref[p, i, 0, place, :] = made[begin : begin + part, p * width : (p + 1) * width]


def in_proj(x, w, parts, at):
    pieces, rows, depth = x.shape
    chan = w.shape[2]
    width = chan // parts
    if width % 128:
        y = jnp.einsum("ird,kdpc->pikrc", x, w.reshape(3, depth, parts, width), preferred_element_type=F32)
        y = y.astype(BF).reshape(parts, pieces, 3, parts, rows // parts, width)
        order = lax.bitwise_xor(jnp.arange(parts, dtype=jnp.int32), at)
        return jnp.take(y, order, axis=3).reshape(parts, pieces, 3, rows, width)
    tile = chan if pieces * rows <= 256 else max(width, chan // 2)
    each = tile // width
    return pl.pallas_call(
        functools.partial(in_proj_body, parts=parts),
        grid_spec=pltpu.PrefetchScalarGridSpec(
            num_scalar_prefetch=1,
            grid=(3, chan // tile),
            in_specs=[
                pl.BlockSpec((pieces * rows, depth), lambda k, p, s: (0, 0)),
                pl.BlockSpec((1, depth, tile), lambda k, p, s: (k, 0, p)),
            ],
            out_specs=pl.BlockSpec((each, pieces, 1, rows, width), lambda k, p, s: (p, 0, k, 0, 0)),
        ),
        out_shape=jax.ShapeDtypeStruct((parts, pieces, 3, rows, width), BF),
        compiler_params=pltpu.CompilerParams(vmem_limit_bytes=48 * MIB),
        cost_estimate=pl.CostEstimate(
            flops=2 * pieces * rows * depth * 3 * chan,
            bytes_accessed=2 * (3 * depth * chan + pieces * rows * (depth + 3 * chan)),
            transcendentals=0,
        ),
    )(at.reshape(1), x.reshape(pieces * rows, depth), w)


def toeplitz_body(taps_ref, o_ref):
    groups = taps_ref.shape[1]
    for g in range(groups):
        row = jnp.broadcast_to(taps_ref[0, pl.ds(g, 1), :], (KL, 2 * KL))
        o_ref[0, pl.ds(g * KL, KL), :] = pltpu.roll(row, 0, 1, stride=1, stride_axis=0).astype(BF)


def toeplitz(taps):
    tiles, groups, _ = taps.shape
    return pl.pallas_call(
        toeplitz_body,
        grid=(tiles,),
        in_specs=[pl.BlockSpec((1, groups, 2 * KL), lambda c: (c, 0, 0))],
        out_specs=pl.BlockSpec((1, groups * KL, 2 * KL), lambda c: (c, 0, 0)),
        out_shape=jax.ShapeDtypeStruct((tiles, groups * KL, 2 * KL), BF),
        cost_estimate=pl.CostEstimate(flops=0, bytes_accessed=0, transcendentals=0),
    )(taps)


def conv_body(groups, base_ref, a_ref, b_ref, pos_ref, short_ref, toep_ref, *refs):
    outs, (proj, prod) = refs[:-2], refs[-2:]
    shards = outs[0].shape[0]
    rows, lanes = a_ref.shape[2], a_ref.shape[3]
    part = rows // shards
    shard_len = sum(o.shape[1] for o in outs)
    near = a_ref.shape[0]
    for k in range(3):
        proj[k, pl.ds(0, 8), :] = jnp.zeros((8, lanes), F32)
    for i in range(near + b_ref.shape[0]):
        y_ref, at = (a_ref, i) if i < near else (b_ref, i - near)
        others = b_ref.shape[0] // near
        apart = i if i < near else (1 + at % others) * near + at // others
        offset = lax.bitwise_xor(jnp.int32(apart), base_ref[0]) * part + 8
        for t in range(shards):
            place = pl.ds(pl.multiple_of(offset + t * shard_len, 8), part)
            for k in range(3):
                proj[k, place, :] = y_ref[at, k, pl.ds(t * part, part), :].astype(F32)
    prod[pl.ds(0, KL), :] = jnp.zeros((KL, lanes), BF)
    lag = (
        KL
        + lax.broadcasted_iota(jnp.int32, (KL, 2 * KL), 0)
        - lax.broadcasted_iota(jnp.int32, (KL, 2 * KL), 1)
    )
    group_of = lax.broadcasted_iota(jnp.int32, (KL, lanes), 1) // GROUP

    def block(start):
        pos = pos_ref[pl.ds(start, KL), :]
        pos_lanes = jnp.broadcast_to(pos, (KL, lanes))
        sums = [None, None, None]
        for j in range(KS):
            keep = pos_lanes >= j
            for k in range(3):
                source = proj[k, pl.ds(start + (8 - j), KL), :]
                term = short_ref[j, k : k + 1, :] * source
                if j == 0:
                    sums[k] = term
                else:
                    sums[k] = sums[k] + jnp.where(keep, term, 0.0)
        prod[pl.ds(start + KL, KL), :] = (sums[1] * sums[2]).astype(BF)
        source = prod[pl.ds(start, 2 * KL), :]
        linked = (lag <= jnp.broadcast_to(pos, (KL, 2 * KL))) & (lag >= 0)
        linked = linked.astype(F32).astype(BF)
        total = jnp.zeros((KL, lanes), F32)
        for g in range(groups):
            masked = toep_ref[0, pl.ds(g * KL, KL), :] * linked
            made = jnp.dot(masked, source, preferred_element_type=F32)
            total = jnp.where(group_of == g, made, total)
        return (sums[0] * total).astype(BF)

    def shard(t, carry):
        for b in range(shard_len // KL):
            gated = block(pl.multiple_of(t * shard_len + b * KL, KL))
            begin = 0
            for o in outs:
                end = begin + o.shape[1]
                lo, hi = max(begin, b * KL), min(end, b * KL + KL)
                if lo < hi:
                    o[t, lo - begin : hi - begin, :] = gated[lo - b * KL : hi - b * KL]
                begin = end
        return carry

    lax.fori_loop(0, shards, shard, 0)


def convolve(first, second, position, short, matrices, shards, base, splits):
    pieces, _, rows, chan = second.shape
    near = first.shape[0]
    pieces += near
    seq_len = pieces * rows
    tile = chan // matrices.shape[0]
    groups = tile // GROUP
    return pl.pallas_call(
        functools.partial(conv_body, groups),
        grid_spec=pltpu.PrefetchScalarGridSpec(
            num_scalar_prefetch=1,
            grid=(chan // tile,),
            in_specs=[
                pl.BlockSpec((near, 3, rows, tile), lambda c, s: (0, 0, 0, c)),
                pl.BlockSpec((pieces - near, 3, rows, tile), lambda c, s: (0, 0, 0, c)),
                pl.BlockSpec((seq_len, 1), lambda c, s: (0, 0)),
                pl.BlockSpec((KS, 3, tile), lambda c, s: (0, 0, c)),
                pl.BlockSpec((1, groups * KL, 2 * KL), lambda c, s: (c, 0, 0)),
            ],
            out_specs=[pl.BlockSpec((shards, n, tile), lambda c, s: (0, 0, c)) for n in splits],
            scratch_shapes=[
                pltpu.VMEM((3, seq_len + 8, tile), F32),
                pltpu.VMEM((seq_len + KL, tile), BF),
            ],
        ),
        out_shape=[jax.ShapeDtypeStruct((shards, n, chan), BF) for n in splits],
        compiler_params=pltpu.CompilerParams(vmem_limit_bytes=62 * MIB),
        cost_estimate=pl.CostEstimate(
            flops=2 * seq_len * chan * 2 * KL * groups,
            bytes_accessed=seq_len * chan * 8,
            transcendentals=0,
        ),
    )(base, first, second, position, short, matrices)


def out_proj_body(place_ref, g_ref, w_ref, o_ref):
    parts, seq_len = g_ref.shape[0], g_ref.shape[1]
    pieces, rows = o_ref.shape[0], o_ref.shape[1]

    def product(at):
        left = jnp.concatenate([g_ref[p, at, :] for p in range(parts)], axis=1)
        return jnp.dot(left, w_ref[...], preferred_element_type=F32).astype(BF)

    if pieces * rows == seq_len:
        made = product(pl.ds(0, seq_len))
        for t in range(pieces):
            o_ref[place_ref[1 + pieces + t]] = made[t * rows : (t + 1) * rows]
    else:
        for e in range(pieces):
            at = pl.multiple_of(place_ref[1 + e] * rows, rows)
            o_ref[e] = product(pl.ds(at, rows))


def out_proj(g, w, place, pieces, rows, cols):
    parts, seq_len, width = g.shape
    tile = min(512, cols)
    per = cols // tile
    return pl.pallas_call(
        out_proj_body,
        grid_spec=pltpu.PrefetchScalarGridSpec(
            num_scalar_prefetch=1,
            grid=(per,),
            in_specs=[
                pl.BlockSpec((parts, seq_len, width), lambda n, s: (0, 0, 0)),
                pl.BlockSpec((parts * width, tile), lambda n, s: (0, s[0] * per + n)),
            ],
            out_specs=pl.BlockSpec((pieces, rows, tile), lambda n, s: (0, 0, n)),
        ),
        out_shape=jax.ShapeDtypeStruct((pieces, rows, cols), BF),
        compiler_params=pltpu.CompilerParams(vmem_limit_bytes=48 * MIB),
        cost_estimate=pl.CostEstimate(
            flops=2 * pieces * rows * parts * width * cols * 16,
            bytes_accessed=2 * (parts * width * (seq_len + cols) + pieces * rows * cols),
            transcendentals=0,
        ),
    )(place, g, w)


def shards(tokens, norm_gain, in_weight, short_filter, long_filter, out_weight, segment_ids):
    n_seq, n_fsdp, n_tp = (lax.axis_size(a) for a in ("seq", "fsdp", "tp"))
    plane = n_fsdp * n_tp
    rows_dev, width_all = tokens.shape
    depth = in_weight.shape[1]
    chan_dev = in_weight.shape[2]
    z, f, c = (lax.axis_index(a) for a in ("seq", "fsdp", "tp"))
    q = f * n_tp + c
    rows = rows_dev // plane
    seq_len = segment_ids.shape[0]

    def swap_core(v):
        return lax.ppermute(v, "tp", [(i, i ^ 1) for i in range(n_tp)])

    def swap_chip(v, e):
        return lax.ppermute(v, "fsdp", [(i, i ^ e) for i in range(n_fsdp)])

    chan = chan_dev // n_seq
    groups = chan // GROUP
    taps = lax.dynamic_slice_in_dim(long_filter, z * groups, groups, 1)
    taps = jnp.concatenate(
        [jnp.zeros((1, groups), F32), taps[::-1], jnp.zeros((KL - 1, groups), F32)], axis=0
    ).T
    tiles = chan // 128 if chan % 128 == 0 else 1
    matrices = toeplitz(taps.reshape(tiles, groups // tiles, 2 * KL))
    def swap_shard(v, e):
        return lax.ppermute(v, "seq", [(i, i ^ e) for i in range(n_seq)])

    split = norm(tokens, norm_gain, jnp.stack([q, z]).astype(jnp.int32), rows, n_seq)
    own = jnp.concatenate([split[0]] + [swap_shard(split[e], e) for e in range(1, n_seq)])
    near = swap_core(own)
    far = [swap_chip(own, e) for e in range(1, n_fsdp)]
    first = in_proj(jnp.stack([own, near]), in_weight, n_seq, z)
    got_first = lax.psum_scatter(first, "seq", scatter_dimension=0)
    far, first = lax.optimization_barrier((far, first))
    far = jnp.stack(far)
    both = jnp.concatenate([far, swap_core(far)])
    both, matrices = lax.optimization_barrier((both, matrices))
    second = in_proj(both, in_weight, n_seq, z)
    got_second = lax.psum_scatter(second, "seq", scatter_dimension=0)

    at = jnp.arange(seq_len, dtype=jnp.int32)
    earlier = (segment_ids[None, :] == segment_ids[:, None]) & (at[None, :] < at[:, None])
    position = jnp.sum(earlier.astype(jnp.int32), axis=1, keepdims=True)
    short = lax.dynamic_slice_in_dim(short_filter, z * chan, chan, 2)
    splits = (SPLIT, rows_dev - SPLIT)
    base = q.astype(jnp.int32).reshape(1)
    gated = convolve(got_first, got_second, position, short, matrices, n_seq, base, splits)

    halves = plane // n_seq
    cols = out_weight.shape[1] // halves

    def block_of(p):
        return lax.bitwise_xor(p // halves, z)

    def place_for(core):
        piece = [lax.bitwise_xor(f, e) * n_tp + core for e in range(n_fsdp)]
        blocks = [block_of(p) for p in piece]
        inverse = [lax.bitwise_xor(lax.bitwise_xor(t, z) * halves // n_tp, f) for t in range(n_fsdp)]
        return jnp.stack([piece[0] % halves] + blocks + inverse).astype(jnp.int32)

    place_away, place_keep = place_for(1 - c), place_for(c)

    def flat(s, p):
        return (p // n_tp * n_seq + s) * n_tp + p % n_tp

    pairs = [
        (flat(s, p), flat((p // halves) ^ s, s * halves + p % halves))
        for s in range(n_seq)
        for p in range(plane)
    ]
    placed, sends = [], None
    gathers = [lax.all_gather(part, "seq", axis=0) for part in gated]
    for gathered, count in zip(gathers, splits):
        if sends is not None:
            gathered, sends = lax.optimization_barrier((gathered, sends))
            placed[-1] = sends
        gathered = gathered.reshape(n_seq, n_seq * count, chan)
        away = out_proj(gathered, out_weight, place_away, n_fsdp, count, cols)
        near = swap_core(away)
        keep = out_proj(gathered, out_weight, place_keep, n_fsdp, count, cols)
        total = keep[0].astype(F32) + near[0].astype(F32)
        sends = [(keep[e].astype(F32) + near[e].astype(F32)).astype(BF) for e in range(1, n_fsdp)]
        for e in range(1, n_fsdp):
            total = total + swap_chip(sends[e - 1], e).astype(F32)
        sends = total.astype(BF)
        placed.append(sends)
    placed = [lax.ppermute(p, ("fsdp", "seq", "tp"), pairs) for p in placed]
    residual = lax.optimization_barrier(lax.dynamic_slice_in_dim(tokens, q * cols, cols, 1))
    return (residual.astype(F32) + jnp.concatenate(placed, axis=0).astype(F32)).astype(BF)


def solution(mesh):
    return jax.shard_map(
        shards,
        mesh=mesh,
        in_specs=(
            P("seq", None),
            P(),
            P(None, "seq", ("fsdp", "tp")),
            P(None, None, ("fsdp", "tp")),
            P(None, ("fsdp", "tp")),
            P(("fsdp", "tp"), "seq"),
            P(),
        ),
        out_specs=P("seq", ("fsdp", "tp")),
        check_vma=False,
    )
```

```python
import functools
import jax
import jax.numpy as jnp
from jax import lax
from jax.experimental import pallas as pl
from jax.experimental.pallas import tpu as pltpu
from jax.sharding import PartitionSpec as P

GROUP = 16
SPLIT = 80
KS = 7
KL = 128
BF = jnp.bfloat16
F32 = jnp.float32
MIB = 1024 * 1024


def norm_body(row_ref, shard_ref, t_ref, gain_ref, *refs):
    outs, held = refs[:-1], refs[-1]
    wide = t_ref[...].astype(F32)
    squares = jnp.mean(wide * wide, axis=1, keepdims=True)
    normed = (wide * lax.rsqrt(squares + 1e-06) * gain_ref[...]).astype(BF)
    depth = held.shape[2]
    for p in range(held.shape[0]):
        held[p] = normed[:, p * depth : (p + 1) * depth]
    for e, o in enumerate(outs):
        o[...] = held[lax.bitwise_xor(shard_ref[0], e)]


def norm(tokens, gain, at, shard, rows, parts):
    width = tokens.shape[1]
    depth = width // parts
    return pl.pallas_call(
        norm_body,
        grid_spec=pltpu.PrefetchScalarGridSpec(
            num_scalar_prefetch=2,
            grid=(1,),
            in_specs=[
                pl.BlockSpec((rows, width), lambda i, a, s: (a[0], 0)),
                pl.BlockSpec((1, width), lambda i, a, s: (0, 0)),
            ],
            out_specs=[pl.BlockSpec((rows, depth), lambda i, a, s: (0, 0))] * parts,
            scratch_shapes=[pltpu.VMEM((parts, rows, depth), BF)],
        ),
        out_shape=[jax.ShapeDtypeStruct((rows, depth), BF)] * parts,
        compiler_params=pltpu.CompilerParams(vmem_limit_bytes=62 * MIB),
    )(at.reshape(1), shard.reshape(1), tokens, gain.reshape(1, width))


def in_proj_body(at_ref, x_ref, w_ref, o_ref, *, parts):
    each, pieces, rows, width = o_ref.shape[0], o_ref.shape[1], o_ref.shape[3], o_ref.shape[4]
    made = jnp.dot(x_ref[...], w_ref[0], preferred_element_type=F32).astype(BF)
    part = rows // parts
    for e in range(parts):
        place = pl.ds(pl.multiple_of(lax.bitwise_xor(at_ref[0], e) * part, part), part)
        for i in range(pieces):
            begin = i * rows + e * part
            for p in range(each):
                o_ref[p, i, 0, place, :] = made[begin : begin + part, p * width : (p + 1) * width]


def in_proj(x, w, parts, at):
    pieces, rows, depth = x.shape
    chan = w.shape[2]
    width = chan // parts
    if width % 128:
        y = jnp.einsum("ird,kdpc->pikrc", x, w.reshape(3, depth, parts, width), preferred_element_type=F32)
        y = y.astype(BF).reshape(parts, pieces, 3, parts, rows // parts, width)
        order = lax.bitwise_xor(jnp.arange(parts, dtype=jnp.int32), at)
        return jnp.take(y, order, axis=3).reshape(parts, pieces, 3, rows, width)
    tile = chan if pieces * rows <= 256 else max(width, chan // 2)
    each = tile // width
    return pl.pallas_call(
        functools.partial(in_proj_body, parts=parts),
        grid_spec=pltpu.PrefetchScalarGridSpec(
            num_scalar_prefetch=1,
            grid=(3, chan // tile),
            in_specs=[
                pl.BlockSpec((pieces * rows, depth), lambda k, p, s: (0, 0)),
                pl.BlockSpec((1, depth, tile), lambda k, p, s: (k, 0, p)),
            ],
            out_specs=pl.BlockSpec((each, pieces, 1, rows, width), lambda k, p, s: (p, 0, k, 0, 0)),
        ),
        out_shape=jax.ShapeDtypeStruct((parts, pieces, 3, rows, width), BF),
        compiler_params=pltpu.CompilerParams(vmem_limit_bytes=48 * MIB),
        cost_estimate=pl.CostEstimate(
            flops=2 * pieces * rows * depth * 3 * chan,
            bytes_accessed=2 * (3 * depth * chan + pieces * rows * (depth + 3 * chan)),
            transcendentals=0,
        ),
    )(at.reshape(1), x.reshape(pieces * rows, depth), w)


def toeplitz_body(taps_ref, o_ref):
    groups = taps_ref.shape[1]
    for g in range(groups):
        row = jnp.broadcast_to(taps_ref[0, pl.ds(g, 1), :], (KL, 2 * KL))
        o_ref[0, pl.ds(g * KL, KL), :] = pltpu.roll(row, 0, 1, stride=1, stride_axis=0).astype(BF)


def toeplitz(taps):
    tiles, groups, _ = taps.shape
    return pl.pallas_call(
        toeplitz_body,
        grid=(tiles,),
        in_specs=[pl.BlockSpec((1, groups, 2 * KL), lambda c: (c, 0, 0))],
        out_specs=pl.BlockSpec((1, groups * KL, 2 * KL), lambda c: (c, 0, 0)),
        out_shape=jax.ShapeDtypeStruct((tiles, groups * KL, 2 * KL), BF),
        cost_estimate=pl.CostEstimate(flops=0, bytes_accessed=0, transcendentals=0),
    )(taps)


def conv_body(groups, base_ref, a_ref, b_ref, pos_ref, short_ref, toep_ref, *refs):
    outs, (proj, prod) = refs[:-2], refs[-2:]
    shards = outs[0].shape[0]
    rows, lanes = a_ref.shape[2], a_ref.shape[3]
    part = rows // shards
    shard_len = sum(o.shape[1] for o in outs)
    near = a_ref.shape[0]
    for k in range(3):
        proj[k, pl.ds(0, 8), :] = jnp.zeros((8, lanes), F32)
    for i in range(near + b_ref.shape[0]):
        y_ref, at = (a_ref, i) if i < near else (b_ref, i - near)
        others = b_ref.shape[0] // near
        apart = i if i < near else (1 + at % others) * near + at // others
        offset = lax.bitwise_xor(jnp.int32(apart), base_ref[0]) * part + 8
        for t in range(shards):
            place = pl.ds(pl.multiple_of(offset + t * shard_len, 8), part)
            for k in range(3):
                proj[k, place, :] = y_ref[at, k, pl.ds(t * part, part), :].astype(F32)
    prod[pl.ds(0, KL), :] = jnp.zeros((KL, lanes), BF)
    lag = (
        KL
        + lax.broadcasted_iota(jnp.int32, (KL, 2 * KL), 0)
        - lax.broadcasted_iota(jnp.int32, (KL, 2 * KL), 1)
    )
    group_of = lax.broadcasted_iota(jnp.int32, (KL, lanes), 1) // GROUP

    def block(start):
        pos = pos_ref[pl.ds(start, KL), :]
        pos_lanes = jnp.broadcast_to(pos, (KL, lanes))
        sums = [None, None, None]
        for j in range(KS):
            keep = pos_lanes >= j
            for k in range(3):
                source = proj[k, pl.ds(start + (8 - j), KL), :]
                term = short_ref[j, k : k + 1, :] * source
                if j == 0:
                    sums[k] = term
                else:
                    sums[k] = sums[k] + jnp.where(keep, term, 0.0)
        prod[pl.ds(start + KL, KL), :] = (sums[1] * sums[2]).astype(BF)
        source = prod[pl.ds(start, 2 * KL), :]
        linked = (lag <= jnp.broadcast_to(pos, (KL, 2 * KL))) & (lag >= 0)
        linked = linked.astype(F32).astype(BF)
        total = jnp.zeros((KL, lanes), F32)
        for g in range(groups):
            masked = toep_ref[0, pl.ds(g * KL, KL), :] * linked
            made = jnp.dot(masked, source, preferred_element_type=F32)
            total = jnp.where(group_of == g, made, total)
        return (sums[0] * total).astype(BF)

    def shard(t, carry):
        for b in range(shard_len // KL):
            gated = block(pl.multiple_of(t * shard_len + b * KL, KL))
            begin = 0
            for o in outs:
                end = begin + o.shape[1]
                lo, hi = max(begin, b * KL), min(end, b * KL + KL)
                if lo < hi:
                    o[t, lo - begin : hi - begin, :] = gated[lo - b * KL : hi - b * KL]
                begin = end
        return carry

    lax.fori_loop(0, shards, shard, 0)


def convolve(first, second, position, short, matrices, shards, base, splits):
    pieces, _, rows, chan = second.shape
    near = first.shape[0]
    pieces += near
    seq_len = pieces * rows
    tile = chan // matrices.shape[0]
    groups = tile // GROUP
    return pl.pallas_call(
        functools.partial(conv_body, groups),
        grid_spec=pltpu.PrefetchScalarGridSpec(
            num_scalar_prefetch=1,
            grid=(chan // tile,),
            in_specs=[
                pl.BlockSpec((near, 3, rows, tile), lambda c, s: (0, 0, 0, c)),
                pl.BlockSpec((pieces - near, 3, rows, tile), lambda c, s: (0, 0, 0, c)),
                pl.BlockSpec((seq_len, 1), lambda c, s: (0, 0)),
                pl.BlockSpec((KS, 3, tile), lambda c, s: (0, 0, c)),
                pl.BlockSpec((1, groups * KL, 2 * KL), lambda c, s: (c, 0, 0)),
            ],
            out_specs=[pl.BlockSpec((shards, n, tile), lambda c, s: (0, 0, c)) for n in splits],
            scratch_shapes=[
                pltpu.VMEM((3, seq_len + 8, tile), F32),
                pltpu.VMEM((seq_len + KL, tile), BF),
            ],
        ),
        out_shape=[jax.ShapeDtypeStruct((shards, n, chan), BF) for n in splits],
        compiler_params=pltpu.CompilerParams(vmem_limit_bytes=62 * MIB),
        cost_estimate=pl.CostEstimate(
            flops=2 * seq_len * chan * 2 * KL * groups,
            bytes_accessed=seq_len * chan * 8,
            transcendentals=0,
        ),
    )(base, first, second, position, short, matrices)


def out_proj_body(place_ref, g_ref, w_ref, o_ref):
    parts, seq_len = g_ref.shape[0], g_ref.shape[1]
    pieces, rows = o_ref.shape[0], o_ref.shape[1]

    def product(at):
        left = jnp.concatenate([g_ref[p, at, :] for p in range(parts)], axis=1)
        return jnp.dot(left, w_ref[...], preferred_element_type=F32).astype(BF)

    if pieces * rows == seq_len:
        made = product(pl.ds(0, seq_len))
        for t in range(pieces):
            o_ref[place_ref[1 + pieces + t]] = made[t * rows : (t + 1) * rows]
    else:
        for e in range(pieces):
            at = pl.multiple_of(place_ref[1 + e] * rows, rows)
            o_ref[e] = product(pl.ds(at, rows))


def out_proj(g, w, place, pieces, rows, cols):
    parts, seq_len, width = g.shape
    tile = min(1024, cols)
    per = cols // tile
    return pl.pallas_call(
        out_proj_body,
        grid_spec=pltpu.PrefetchScalarGridSpec(
            num_scalar_prefetch=1,
            grid=(per,),
            in_specs=[
                pl.BlockSpec((parts, seq_len, width), lambda n, s: (0, 0, 0)),
                pl.BlockSpec((parts * width, tile), lambda n, s: (0, s[0] * per + n)),
            ],
            out_specs=pl.BlockSpec((pieces, rows, tile), lambda n, s: (0, 0, n)),
        ),
        out_shape=jax.ShapeDtypeStruct((pieces, rows, cols), BF),
        compiler_params=pltpu.CompilerParams(vmem_limit_bytes=48 * MIB),
        cost_estimate=pl.CostEstimate(
            flops=2 * pieces * rows * parts * width * cols * 16,
            bytes_accessed=2 * (parts * width * (seq_len + cols) + pieces * rows * cols),
            transcendentals=0,
        ),
    )(place, g, w)


def shards(tokens, norm_gain, in_weight, short_filter, long_filter, out_weight, segment_ids):
    n_seq, n_fsdp, n_tp = (lax.axis_size(a) for a in ("seq", "fsdp", "tp"))
    plane = n_fsdp * n_tp
    rows_dev, width_all = tokens.shape
    depth = in_weight.shape[1]
    chan_dev = in_weight.shape[2]
    z, f, c = (lax.axis_index(a) for a in ("seq", "fsdp", "tp"))
    q = f * n_tp + c
    rows = rows_dev // plane
    seq_len = segment_ids.shape[0]

    def swap_core(v):
        return lax.ppermute(v, "tp", [(i, i ^ 1) for i in range(n_tp)])

    def swap_chip(v, e):
        return lax.ppermute(v, "fsdp", [(i, i ^ e) for i in range(n_fsdp)])

    chan = chan_dev // n_seq
    groups = chan // GROUP
    taps = lax.dynamic_slice_in_dim(long_filter, z * groups, groups, 1)
    taps = jnp.concatenate(
        [jnp.zeros((1, groups), F32), taps[::-1], jnp.zeros((KL - 1, groups), F32)], axis=0
    ).T
    tiles = chan // 128 if chan % 128 == 0 else 1
    matrices = toeplitz(taps.reshape(tiles, groups // tiles, 2 * KL))
    def swap_shard(v, e):
        return lax.ppermute(v, "seq", [(i, i ^ e) for i in range(n_seq)])

    split = norm(tokens, norm_gain, q.astype(jnp.int32), z.astype(jnp.int32), rows, n_seq)
    own = jnp.concatenate([split[0]] + [swap_shard(split[e], e) for e in range(1, n_seq)])
    near = swap_core(own)
    far = [swap_chip(own, e) for e in range(1, n_fsdp)]
    first = in_proj(jnp.stack([own, near]), in_weight, n_seq, z)
    got_first = lax.psum_scatter(first, "seq", scatter_dimension=0)
    far, first = lax.optimization_barrier((far, first))
    far = jnp.stack(far)
    both = jnp.concatenate([far, swap_core(far)])
    both, matrices = lax.optimization_barrier((both, matrices))
    second = in_proj(both, in_weight, n_seq, z)
    got_second = lax.psum_scatter(second, "seq", scatter_dimension=0)

    at = jnp.arange(seq_len, dtype=jnp.int32)
    earlier = (segment_ids[None, :] == segment_ids[:, None]) & (at[None, :] < at[:, None])
    position = jnp.sum(earlier.astype(jnp.int32), axis=1, keepdims=True)
    short = lax.dynamic_slice_in_dim(short_filter, z * chan, chan, 2)
    splits = (SPLIT, rows_dev - SPLIT)
    base = q.astype(jnp.int32).reshape(1)
    gated = convolve(got_first, got_second, position, short, matrices, n_seq, base, splits)

    halves = plane // n_seq
    cols = out_weight.shape[1] // halves

    def spread(s):
        return (((s ^ (s >> 1)) & 1) << 1) | (s >> 1) if n_seq == 4 else s

    def block_of(p):
        return (p // halves) ^ spread(z)

    def place_for(core):
        piece = [lax.bitwise_xor(f, e) * n_tp + core for e in range(n_fsdp)]
        blocks = [block_of(p) for p in piece]
        inverse = [((t ^ spread(z)) * halves // n_tp) ^ f for t in range(n_fsdp)]
        return jnp.stack([piece[0] % halves] + blocks + inverse).astype(jnp.int32)

    place_away, place_keep = place_for(1 - c), place_for(c)

    def flat(s, p):
        return (p // n_tp * n_seq + s) * n_tp + p % n_tp

    pairs = [
        (flat(s, p), flat((p // halves) ^ spread(s), s * halves + p % halves))
        for s in range(n_seq)
        for p in range(plane)
    ]
    placed, sends = [], None
    gathers = [lax.all_gather(part, "seq", axis=0) for part in gated]
    for gathered, count in zip(gathers, splits):
        if sends is not None:
            gathered, sends = lax.optimization_barrier((gathered, sends))
            placed[-1] = sends
        gathered = gathered.reshape(n_seq, n_seq * count, chan)
        away = out_proj(gathered, out_weight, place_away, n_fsdp, count, cols)
        near = swap_core(away)
        keep = out_proj(gathered, out_weight, place_keep, n_fsdp, count, cols)
        total = keep[0].astype(F32) + near[0].astype(F32)
        sends = [(keep[e].astype(F32) + near[e].astype(F32)).astype(BF) for e in range(1, n_fsdp)]
        for e in range(1, n_fsdp):
            total = total + swap_chip(sends[e - 1], e).astype(F32)
        sends = total.astype(BF)
        placed.append(sends)
    placed = [lax.ppermute(p, ("fsdp", "seq", "tp"), pairs) for p in placed]
    residual = lax.optimization_barrier(lax.dynamic_slice_in_dim(tokens, q * cols, cols, 1))
    return (residual.astype(F32) + jnp.concatenate(placed, axis=0).astype(F32)).astype(BF)


def solution(mesh):
    return jax.shard_map(
        shards,
        mesh=mesh,
        in_specs=(
            P("seq", None),
            P(),
            P(None, "seq", ("fsdp", "tp")),
            P(None, None, ("fsdp", "tp")),
            P(None, ("fsdp", "tp")),
            P(("fsdp", "tp"), "seq"),
            P(),
        ),
        out_specs=P("seq", ("fsdp", "tp")),
        check_vma=False,
    )
```

```python
import functools
import jax
import jax.numpy as jnp
from jax import lax
from jax.experimental import pallas as pl
from jax.experimental.pallas import tpu as pltpu
from jax.sharding import PartitionSpec as P

GROUP = 16
SPLIT = 80
KS = 7
KL = 128
BF = jnp.bfloat16
F32 = jnp.float32
MIB = 1024 * 1024


def norm_body(row_ref, shard_ref, t_ref, gain_ref, *refs):
    outs, held = refs[:-1], refs[-1]
    wide = t_ref[...].astype(F32)
    squares = jnp.mean(wide * wide, axis=1, keepdims=True)
    normed = (wide * lax.rsqrt(squares + 1e-06) * gain_ref[...]).astype(BF)
    depth = held.shape[2]
    for p in range(held.shape[0]):
        held[p] = normed[:, p * depth : (p + 1) * depth]
    for e, o in enumerate(outs):
        o[...] = held[lax.bitwise_xor(shard_ref[0], e)]


def norm(tokens, gain, at, shard, rows, parts):
    width = tokens.shape[1]
    depth = width // parts
    return pl.pallas_call(
        norm_body,
        grid_spec=pltpu.PrefetchScalarGridSpec(
            num_scalar_prefetch=2,
            grid=(1,),
            in_specs=[
                pl.BlockSpec((rows, width), lambda i, a, s: (a[0], 0)),
                pl.BlockSpec((1, width), lambda i, a, s: (0, 0)),
            ],
            out_specs=[pl.BlockSpec((rows, depth), lambda i, a, s: (0, 0))] * parts,
            scratch_shapes=[pltpu.VMEM((parts, rows, depth), BF)],
        ),
        out_shape=[jax.ShapeDtypeStruct((rows, depth), BF)] * parts,
        compiler_params=pltpu.CompilerParams(vmem_limit_bytes=62 * MIB),
    )(at.reshape(1), shard.reshape(1), tokens, gain.reshape(1, width))


def in_proj_body(at_ref, x_ref, w_ref, o_ref, *, parts):
    each, pieces, rows, width = o_ref.shape[0], o_ref.shape[1], o_ref.shape[3], o_ref.shape[4]
    made = jnp.dot(x_ref[...], w_ref[0], preferred_element_type=F32).astype(BF)
    part = rows // parts
    for e in range(parts):
        place = pl.ds(pl.multiple_of(lax.bitwise_xor(at_ref[0], e) * part, part), part)
        for i in range(pieces):
            begin = i * rows + e * part
            for p in range(each):
                o_ref[p, i, 0, place, :] = made[begin : begin + part, p * width : (p + 1) * width]


def in_proj(x, w, parts, at):
    pieces, rows, depth = x.shape
    chan = w.shape[2]
    width = chan // parts
    if width % 128:
        y = jnp.einsum("ird,kdpc->pikrc", x, w.reshape(3, depth, parts, width), preferred_element_type=F32)
        y = y.astype(BF).reshape(parts, pieces, 3, parts, rows // parts, width)
        order = lax.bitwise_xor(jnp.arange(parts, dtype=jnp.int32), at)
        return jnp.take(y, order, axis=3).reshape(parts, pieces, 3, rows, width)
    tile = chan if pieces * rows <= 256 else max(width, chan // 2)
    each = tile // width
    return pl.pallas_call(
        functools.partial(in_proj_body, parts=parts),
        grid_spec=pltpu.PrefetchScalarGridSpec(
            num_scalar_prefetch=1,
            grid=(3, chan // tile),
            in_specs=[
                pl.BlockSpec((pieces * rows, depth), lambda k, p, s: (0, 0)),
                pl.BlockSpec((1, depth, tile), lambda k, p, s: (k, 0, p)),
            ],
            out_specs=pl.BlockSpec((each, pieces, 1, rows, width), lambda k, p, s: (p, 0, k, 0, 0)),
        ),
        out_shape=jax.ShapeDtypeStruct((parts, pieces, 3, rows, width), BF),
        compiler_params=pltpu.CompilerParams(vmem_limit_bytes=48 * MIB),
        cost_estimate=pl.CostEstimate(
            flops=2 * pieces * rows * depth * 3 * chan,
            bytes_accessed=2 * (3 * depth * chan + pieces * rows * (depth + 3 * chan)),
            transcendentals=0,
        ),
    )(at.reshape(1), x.reshape(pieces * rows, depth), w)


def toeplitz_body(taps_ref, o_ref):
    groups = taps_ref.shape[1]
    for g in range(groups):
        row = jnp.broadcast_to(taps_ref[0, pl.ds(g, 1), :], (KL, 2 * KL))
        o_ref[0, pl.ds(g * KL, KL), :] = pltpu.roll(row, 0, 1, stride=1, stride_axis=0).astype(BF)


def toeplitz(taps):
    tiles, groups, _ = taps.shape
    return pl.pallas_call(
        toeplitz_body,
        grid=(tiles,),
        in_specs=[pl.BlockSpec((1, groups, 2 * KL), lambda c: (c, 0, 0))],
        out_specs=pl.BlockSpec((1, groups * KL, 2 * KL), lambda c: (c, 0, 0)),
        out_shape=jax.ShapeDtypeStruct((tiles, groups * KL, 2 * KL), BF),
        cost_estimate=pl.CostEstimate(flops=0, bytes_accessed=0, transcendentals=0),
    )(taps)


def conv_body(groups, base_ref, a_ref, b_ref, pos_ref, short_ref, toep_ref, *refs):
    outs, (proj, prod) = refs[:-2], refs[-2:]
    shards = outs[0].shape[0]
    rows, lanes = a_ref.shape[2], a_ref.shape[3]
    part = rows // shards
    shard_len = sum(o.shape[1] for o in outs)
    near = a_ref.shape[0]
    for k in range(3):
        proj[k, pl.ds(0, 8), :] = jnp.zeros((8, lanes), F32)
    for i in range(near + b_ref.shape[0]):
        y_ref, at = (a_ref, i) if i < near else (b_ref, i - near)
        others = b_ref.shape[0] // near
        apart = i if i < near else (1 + at % others) * near + at // others
        offset = lax.bitwise_xor(jnp.int32(apart), base_ref[0]) * part + 8
        for t in range(shards):
            place = pl.ds(pl.multiple_of(offset + t * shard_len, 8), part)
            for k in range(3):
                proj[k, place, :] = y_ref[at, k, pl.ds(t * part, part), :].astype(F32)
    prod[pl.ds(0, KL), :] = jnp.zeros((KL, lanes), BF)
    lag = (
        KL
        + lax.broadcasted_iota(jnp.int32, (KL, 2 * KL), 0)
        - lax.broadcasted_iota(jnp.int32, (KL, 2 * KL), 1)
    )
    group_of = lax.broadcasted_iota(jnp.int32, (KL, lanes), 1) // GROUP

    def block(start):
        pos = pos_ref[pl.ds(start, KL), :]
        pos_lanes = jnp.broadcast_to(pos, (KL, lanes))
        sums = [None, None, None]
        for j in range(KS):
            keep = pos_lanes >= j
            for k in range(3):
                source = proj[k, pl.ds(start + (8 - j), KL), :]
                term = short_ref[j, k : k + 1, :] * source
                if j == 0:
                    sums[k] = term
                else:
                    sums[k] = sums[k] + jnp.where(keep, term, 0.0)
        prod[pl.ds(start + KL, KL), :] = (sums[1] * sums[2]).astype(BF)
        source = prod[pl.ds(start, 2 * KL), :]
        linked = (lag <= jnp.broadcast_to(pos, (KL, 2 * KL))) & (lag >= 0)
        linked = linked.astype(F32).astype(BF)
        total = jnp.zeros((KL, lanes), F32)
        for g in range(groups):
            masked = toep_ref[0, pl.ds(g * KL, KL), :] * linked
            made = jnp.dot(masked, source, preferred_element_type=F32)
            total = jnp.where(group_of == g, made, total)
        return (sums[0] * total).astype(BF)

    def shard(t, carry):
        for b in range(shard_len // KL):
            gated = block(pl.multiple_of(t * shard_len + b * KL, KL))
            begin = 0
            for o in outs:
                end = begin + o.shape[1]
                lo, hi = max(begin, b * KL), min(end, b * KL + KL)
                if lo < hi:
                    o[t, lo - begin : hi - begin, :] = gated[lo - b * KL : hi - b * KL]
                begin = end
        return carry

    lax.fori_loop(0, shards, shard, 0, unroll=4)


def convolve(first, second, position, short, matrices, shards, base, splits):
    pieces, _, rows, chan = second.shape
    near = first.shape[0]
    pieces += near
    seq_len = pieces * rows
    tile = chan // matrices.shape[0]
    groups = tile // GROUP
    return pl.pallas_call(
        functools.partial(conv_body, groups),
        grid_spec=pltpu.PrefetchScalarGridSpec(
            num_scalar_prefetch=1,
            grid=(chan // tile,),
            in_specs=[
                pl.BlockSpec((near, 3, rows, tile), lambda c, s: (0, 0, 0, c)),
                pl.BlockSpec((pieces - near, 3, rows, tile), lambda c, s: (0, 0, 0, c)),
                pl.BlockSpec((seq_len, 1), lambda c, s: (0, 0)),
                pl.BlockSpec((KS, 3, tile), lambda c, s: (0, 0, c)),
                pl.BlockSpec((1, groups * KL, 2 * KL), lambda c, s: (c, 0, 0)),
            ],
            out_specs=[pl.BlockSpec((shards, n, tile), lambda c, s: (0, 0, c)) for n in splits],
            scratch_shapes=[
                pltpu.VMEM((3, seq_len + 8, tile), F32),
                pltpu.VMEM((seq_len + KL, tile), BF),
            ],
        ),
        out_shape=[jax.ShapeDtypeStruct((shards, n, chan), BF) for n in splits],
        compiler_params=pltpu.CompilerParams(vmem_limit_bytes=62 * MIB),
        cost_estimate=pl.CostEstimate(
            flops=2 * seq_len * chan * 2 * KL * groups,
            bytes_accessed=seq_len * chan * 8,
            transcendentals=0,
        ),
    )(base, first, second, position, short, matrices)


def out_proj_body(place_ref, g_ref, w_ref, o_ref):
    parts, seq_len = g_ref.shape[0], g_ref.shape[1]
    pieces, rows = o_ref.shape[0], o_ref.shape[1]

    def product(at):
        left = jnp.concatenate([g_ref[p, at, :] for p in range(parts)], axis=1)
        return jnp.dot(left, w_ref[...], preferred_element_type=F32).astype(BF)

    if pieces * rows == seq_len:
        made = product(pl.ds(0, seq_len))
        for t in range(pieces):
            o_ref[place_ref[1 + pieces + t]] = made[t * rows : (t + 1) * rows]
    else:
        for e in range(pieces):
            at = pl.multiple_of(place_ref[1 + e] * rows, rows)
            o_ref[e] = product(pl.ds(at, rows))


def out_proj(g, w, place, pieces, rows, cols):
    parts, seq_len, width = g.shape
    tile = min(1024, cols)
    per = cols // tile
    return pl.pallas_call(
        out_proj_body,
        grid_spec=pltpu.PrefetchScalarGridSpec(
            num_scalar_prefetch=1,
            grid=(per,),
            in_specs=[
                pl.BlockSpec((parts, seq_len, width), lambda n, s: (0, 0, 0)),
                pl.BlockSpec((parts * width, tile), lambda n, s: (0, s[0] * per + n)),
            ],
            out_specs=pl.BlockSpec((pieces, rows, tile), lambda n, s: (0, 0, n)),
        ),
        out_shape=jax.ShapeDtypeStruct((pieces, rows, cols), BF),
        compiler_params=pltpu.CompilerParams(vmem_limit_bytes=48 * MIB),
        cost_estimate=pl.CostEstimate(
            flops=2 * pieces * rows * parts * width * cols * 16,
            bytes_accessed=2 * (parts * width * (seq_len + cols) + pieces * rows * cols),
            transcendentals=0,
        ),
    )(place, g, w)


def shards(tokens, norm_gain, in_weight, short_filter, long_filter, out_weight, segment_ids):
    n_seq, n_fsdp, n_tp = (lax.axis_size(a) for a in ("seq", "fsdp", "tp"))
    plane = n_fsdp * n_tp
    rows_dev, width_all = tokens.shape
    depth = in_weight.shape[1]
    chan_dev = in_weight.shape[2]
    z, f, c = (lax.axis_index(a) for a in ("seq", "fsdp", "tp"))
    q = f * n_tp + c
    rows = rows_dev // plane
    seq_len = segment_ids.shape[0]

    def swap_core(v):
        return lax.ppermute(v, "tp", [(i, i ^ 1) for i in range(n_tp)])

    def swap_chip(v, e):
        return lax.ppermute(v, "fsdp", [(i, i ^ e) for i in range(n_fsdp)])

    chan = chan_dev // n_seq
    groups = chan // GROUP
    taps = lax.dynamic_slice_in_dim(long_filter, z * groups, groups, 1)
    taps = jnp.concatenate(
        [jnp.zeros((1, groups), F32), taps[::-1], jnp.zeros((KL - 1, groups), F32)], axis=0
    ).T
    tiles = chan // 128 if chan % 128 == 0 else 1
    matrices = toeplitz(taps.reshape(tiles, groups // tiles, 2 * KL))
    def swap_shard(v, e):
        return lax.ppermute(v, "seq", [(i, i ^ e) for i in range(n_seq)])

    split = norm(tokens, norm_gain, q.astype(jnp.int32), z.astype(jnp.int32), rows, n_seq)
    own = jnp.concatenate([split[0]] + [swap_shard(split[e], e) for e in range(1, n_seq)])
    near = swap_core(own)
    far = [swap_chip(own, e) for e in range(1, n_fsdp)]
    first = in_proj(jnp.stack([own, near]), in_weight, n_seq, z)
    got_first = lax.psum_scatter(first, "seq", scatter_dimension=0)
    far, first = lax.optimization_barrier((far, first))
    far = jnp.stack(far)
    both = jnp.concatenate([far, swap_core(far)])
    both, matrices = lax.optimization_barrier((both, matrices))
    second = in_proj(both, in_weight, n_seq, z)
    got_second = lax.psum_scatter(second, "seq", scatter_dimension=0)

    at = jnp.arange(seq_len, dtype=jnp.int32)
    earlier = (segment_ids[None, :] == segment_ids[:, None]) & (at[None, :] < at[:, None])
    position = jnp.sum(earlier.astype(jnp.int32), axis=1, keepdims=True)
    short = lax.dynamic_slice_in_dim(short_filter, z * chan, chan, 2)
    splits = (SPLIT, rows_dev - SPLIT)
    base = q.astype(jnp.int32).reshape(1)
    gated = convolve(got_first, got_second, position, short, matrices, n_seq, base, splits)

    halves = plane // n_seq
    cols = out_weight.shape[1] // halves

    def spread(s):
        return (((s ^ (s >> 1)) & 1) << 1) | (s >> 1) if n_seq == 4 else s

    def block_of(p):
        return (p // halves) ^ spread(z)

    def place_for(core):
        piece = [lax.bitwise_xor(f, e) * n_tp + core for e in range(n_fsdp)]
        blocks = [block_of(p) for p in piece]
        inverse = [((t ^ spread(z)) * halves // n_tp) ^ f for t in range(n_fsdp)]
        return jnp.stack([piece[0] % halves] + blocks + inverse).astype(jnp.int32)

    place_away, place_keep = place_for(1 - c), place_for(c)

    def flat(s, p):
        return (p // n_tp * n_seq + s) * n_tp + p % n_tp

    pairs = [
        (flat(s, p), flat((p // halves) ^ spread(s), s * halves + p % halves))
        for s in range(n_seq)
        for p in range(plane)
    ]
    placed, sends = [], None
    gathers = [lax.all_gather(part, "seq", axis=0) for part in gated]
    for gathered, count in zip(gathers, splits):
        if sends is not None:
            gathered, sends = lax.optimization_barrier((gathered, sends))
            placed[-1] = sends
        gathered = gathered.reshape(n_seq, n_seq * count, chan)
        away = out_proj(gathered, out_weight, place_away, n_fsdp, count, cols)
        near = swap_core(away)
        keep = out_proj(gathered, out_weight, place_keep, n_fsdp, count, cols)
        total = keep[0].astype(F32) + near[0].astype(F32)
        sends = [(keep[e].astype(F32) + near[e].astype(F32)).astype(BF) for e in range(1, n_fsdp)]
        for e in range(1, n_fsdp):
            total = total + swap_chip(sends[e - 1], e).astype(F32)
        sends = total.astype(BF)
        placed.append(sends)
    placed = [lax.ppermute(p, ("fsdp", "seq", "tp"), pairs) for p in placed]
    residual = lax.optimization_barrier(lax.dynamic_slice_in_dim(tokens, q * cols, cols, 1))
    return (residual.astype(F32) + jnp.concatenate(placed, axis=0).astype(F32)).astype(BF)


def solution(mesh):
    return jax.shard_map(
        shards,
        mesh=mesh,
        in_specs=(
            P("seq", None),
            P(),
            P(None, "seq", ("fsdp", "tp")),
            P(None, None, ("fsdp", "tp")),
            P(None, ("fsdp", "tp")),
            P(("fsdp", "tp"), "seq"),
            P(),
        ),
        out_specs=P("seq", ("fsdp", "tp")),
        check_vma=False,
    )
```
